128 devices in a mesh: seq: 16 (over z, y_hi, core), chan: 8 (over y_lo, x).
Axes of the slice: x: 4, y: 4 (y_hi: 2, y_lo: 2; y = y_hi * 2 + y_lo), z: 4, core: 2. Of those that a mesh axis runs over, the one named last changes fastest.
Arguments:
- values: bfloat16 [4096, 4096], P('seq', 'chan'), may hold values from -6 to 6
- gates: bfloat16 [4096, 4096], P('seq', 'chan'), may hold values from -6 to 6
- filters: bfloat16 [1024, 4096], P(None, 'chan'), may hold values from -2 to 2
- skip: float32 [4096], P('chan'), may hold values from -4 to 4
- out_weight: bfloat16 [4096, 4096], P(('seq', 'chan')), may hold values from -0.09375 to 0.09375
Outputs:
- projected: bfloat16 [4096, 4096], P(('seq', 'chan'))
The draws below stay inside these ranges and needn't reach their ends.
All inputs are finite; a program needn't handle non-finite values.
Results may differ from the reference program's by a relative error of at most 0.009.
Values may be sent and summed in bfloat16 or wider, within the bound.
A program may use at most 128 MiB of HBM per device.

```python
import math
import jax
import jax.numpy as jnp
from jax import lax

D = 4096
FILT = 1024
TOKENS = 4096


def draw_filters(key, part):
    key_noise, key_rate = jax.random.split(jax.random.fold_in(key, 17))
    lagged = jnp.arange(FILT, dtype=jnp.float32)[:, None]
    noise = jnp.clip(jax.random.normal(key_noise, (FILT, D), jnp.float32), -6.0, 6.0)
    log_rate = jax.random.uniform(key_rate, (1, D), jnp.float32, math.log(0.05 / FILT), math.log(1.0 / 30.0))
    rate = jnp.exp(log_rate)
    scale = jnp.sqrt(jnp.expm1(-2.0 * rate) / jnp.expm1(-2.0 * rate * FILT))
    return (noise * jnp.exp(-rate * lagged) * scale).astype(jnp.bfloat16)


def block_levels(key, dims, cuts, low, top_value):
    level = 1.0
    for axis_at, blocks in cuts:
        steps = jax.random.uniform(jax.random.fold_in(jax.random.fold_in(key, 6), axis_at), (blocks,), jnp.float32, low / len(cuts), top_value / len(cuts))
        level = level * jnp.repeat(jnp.exp(steps), dims[axis_at] // blocks).reshape((-1,) + (1,) * (len(dims) - 1 - axis_at))
    return level


def centred(stream_key, extent, deviation, limit, pieces=(), held_as=jnp.bfloat16):
    gain = block_levels(stream_key, extent, pieces, -0.22, 0.18) if pieces else 1.0
    result = jax.random.normal(stream_key, extent, jnp.float32) * deviation * gain
    return jnp.minimum(jnp.maximum(result, -limit), limit).astype(held_as)


def setup_inputs(seed: int = 0) -> dict:
    keys = jax.random.split(jax.random.key(seed), 6)
    values = centred(keys[0], (TOKENS, D), 1.0, 6.0, ((0, 16), (1, 8)))
    gates = centred(keys[1], (TOKENS, D), 1.0, 6.0, ((0, 16), (1, 8)))
    filters = draw_filters(jax.random.fold_in(keys[5], 71), 0)
    skip = centred(keys[3], (D,), 1.0, 4.0, ((0, 8),), jnp.float32)
    out_weight = centred(keys[4], (D, D), D ** -0.5, 0.09375, ((0, 128),))
    return {"values": values, "gates": gates, "filters": filters, "skip": skip, "out_weight": out_weight}


def reference(values, gates, filters, skip, out_weight):
    length = values.shape[0]
    width = values.shape[1]
    group = math.gcd(width, 512)
    count = width // group
    period = 2 * length

    def split_groups(array):
        return jnp.transpose(array.reshape(array.shape[0], count, group), (1, 0, 2))

    def one_group(operands):
        value_part, gate_part, filter_part, skip_part = operands
        value_float = value_part.astype(jnp.float32)
        spectrum = jnp.fft.rfft(value_float, n=period, axis=0) * jnp.fft.rfft(filter_part.astype(jnp.float32), n=period, axis=0)
        convolved = jnp.fft.irfft(spectrum, n=period, axis=0)[:length]
        filtered = convolved + skip_part[None, :] * value_float
        return (gate_part.astype(jnp.float32) * filtered).astype(jnp.bfloat16)

    gated = lax.map(one_group, (split_groups(values), split_groups(gates), split_groups(filters), skip.reshape(count, group)))
    gated = jnp.transpose(gated, (1, 0, 2)).reshape(length, width)
    return jnp.dot(gated, out_weight, preferred_element_type=jnp.float32).astype(jnp.bfloat16)
```

```python
import numpy as np

import jax
import jax.numpy as jnp
from jax import lax
from jax.sharding import PartitionSpec as P


def dft_tables(block):
    size = 2 * block
    freq = (np.arange(block) + 0.5)[:, None]
    angle = 2.0 * np.pi * freq * np.arange(size)[None, :] / size
    forward = np.concatenate([np.cos(angle), -np.sin(angle)], axis=0)
    late = angle[:, block:]
    backward = np.concatenate([np.cos(late), -np.sin(late)], axis=0).T / block
    return forward, backward


def from_behind(value, axis, steps):
    count = lax.axis_size(axis)
    return lax.ppermute(value, axis, [(source, source + steps) for source in range(count - steps)])


def dot(a, b):
    return jnp.dot(a, b, preferred_element_type=jnp.float32)


def body(values, gates, filters, skip, out_weight):
    block = values.shape[0]
    taps = filters.shape[0] // block
    forward, backward = dft_tables(block)
    forward = jnp.asarray(forward, jnp.bfloat16)
    backward = jnp.asarray(backward, jnp.bfloat16)
    part = lax.all_to_all(out_weight, "chan", split_axis=1, concat_axis=0, tiled=True)
    columns = lax.all_gather(part, "seq", axis=0, tiled=True)
    blocks = [values] + [from_behind(values, "seq", step) for step in range(1, taps + 1)]
    real = 0.0
    imag = 0.0
    for j in range(taps):
        kernel = dot(forward[:, :block], filters[j * block : (j + 1) * block])
        window = dot(forward, jnp.concatenate([blocks[j + 1], blocks[j]], axis=0))
        kr, ki = kernel[:block], kernel[block:]
        wr, wi = window[:block], window[block:]
        real = real + kr * wr - ki * wi
        imag = imag + kr * wi + ki * wr
    spectrum = jnp.concatenate([real, imag], axis=0).astype(jnp.bfloat16)
    filtered = dot(backward, spectrum) + skip[None, :] * values.astype(jnp.float32)
    gated = (gates.astype(jnp.float32) * filtered).astype(jnp.bfloat16)
    rows = lax.all_gather(gated, "chan", axis=1, tiled=True)
    summed = dot(rows, columns).astype(jnp.bfloat16)
    return lax.all_to_all(summed, "chan", split_axis=0, concat_axis=1, tiled=True)


def solution(mesh):
    in_specs = (
        P("seq", "chan"),
        P("seq", "chan"),
        P(None, "chan"),
        P("chan"),
        P(("seq", "chan"), None),
    )
    out_specs = P(("seq", "chan"), None)
    return jax.shard_map(body, mesh=mesh, in_specs=in_specs, out_specs=out_specs, check_vma=False)
```

```python
import functools

import numpy as np

import jax
import jax.numpy as jnp
from jax import lax
from jax.experimental import pallas as pl
from jax.experimental.pallas import tpu as pltpu
from jax.sharding import PartitionSpec as P

MESH = pl.DeviceIdType.MESH
CHUNKS = 2
BLOCK = 256
WIDTH = 512
PART = WIDTH // CHUNKS
TAPS = 4
PEERS = 8
GROUPS = 16
ROWS = 32
HALF = BLOCK // 2
STRIP = 32


def dft_tables(block):
    size = 2 * block
    freq = (np.arange(block) + 0.5)[:, None]
    angle = 2.0 * np.pi * freq * np.arange(size)[None, :] / size
    forward = np.concatenate([np.cos(angle), -np.sin(angle)], axis=0)
    late = angle[:, block:]
    backward = np.concatenate([np.cos(late), -np.sin(late)], axis=0).T / block
    return forward, backward


def dot(a, b):
    return jnp.dot(a, b, preferred_element_type=jnp.float32)


def kernel(
    values, gates, filters, skip, weight, forward, backward, out,
    xbuf, gbuf, fbuf, tables, inverse, kern, zbuf, ybuf, abuf, wbuf, acc, obuf,
    send_sem, recv_sem, local_sem,
):
    s = lax.axis_index("seq")
    c = lax.axis_index("chan")
    z, yh, k = s // 4, (s // 2) % 2, s % 2
    yl, x = c // 4, c % 4

    def seq_at(dz, dyh, dk):
        return ((z + dz + 4) % 4) * 4 + ((yh + dyh) % 2) * 2 + (k + dk) % 2

    def chan_at(dyl, dx):
        return ((yl + dyl) % 2) * 4 + (x + dx + 4) % 4

    def seq_dev(index):
        return {"seq": index, "chan": c}

    def chan_dev(index):
        return {"seq": s, "chan": index}

    z_up, z_down = seq_dev(seq_at(1, 0, 0)), seq_dev(seq_at(-1, 0, 0))
    y_far, mate = seq_dev(seq_at(0, 1, 0)), seq_dev(seq_at(0, 0, 1))
    x_up, x_down = chan_dev(chan_at(0, 1)), chan_dev(chan_at(0, -1))
    y_near = chan_dev(chan_at(1, 0))
    ahead, behind = (s + 2) % GROUPS, (s + GROUPS - 2) % GROUPS

    pending = []

    def send(src, dst, device):
        index = len(pending)
        copy = pltpu.make_async_remote_copy(
            src_ref=src, dst_ref=dst, send_sem=send_sem.at[index], recv_sem=recv_sem.at[index],
            device_id=device, device_id_type=MESH,
        )
        copy.start()
        pending.append(copy)
        return copy

    locals_started = []

    def fetch(src, dst):
        copy = pltpu.make_async_copy(src, dst, local_sem.at[len(locals_started)])
        copy.start()
        locals_started.append(copy)
        return copy

    barrier = pltpu.get_barrier_semaphore()
    sources = [chan_dev((c + i) % PEERS) for i in range(1, PEERS)]
    sources += [z_up, z_down, y_far, mate, seq_dev(behind)]
    for device in sources:
        pl.semaphore_signal(barrier, inc=1, device_id=device, device_id_type=MESH)

    def cols(q):
        return pl.ds(q * PART, PART)

    def lag(n):
        return pl.ds((TAPS - n) * BLOCK, BLOCK)

    get_filters = fetch(filters, fbuf)
    get_forward = fetch(forward, tables)
    get_values = [fetch(values.at[:, cols(q)], xbuf.at[q, lag(0)]) for q in range(CHUNKS)]
    get_backward = fetch(backward, inverse)
    get_gates = fetch(gates, gbuf)

    def wcols(index):
        return pl.ds(pl.multiple_of(index * WIDTH, WIDTH), WIDTH)

    def rows_of(index):
        return pl.ds(pl.multiple_of(index * ROWS, ROWS), ROWS)

    get_weight = fetch(weight.at[:, wcols(c)], wbuf.at[s, rows_of(c)])

    pl.semaphore_wait(barrier, len(sources))

    far, near = [], []
    for q in range(CHUNKS):
        near.append(send(values.at[:, cols(q)], xbuf.at[q, lag(2)], seq_dev(ahead)))
        far.append(send(values.at[:, cols(q)], xbuf.at[q, lag(4)], z_up))
    shares = []
    for i in range(1, PEERS):
        peer = (c + i) % PEERS
        shares.append(send(weight.at[:, wcols(peer)], wbuf.at[s, rows_of(c)], chan_dev(peer)))

    get_filters.wait()
    get_forward.wait()

    def spectrum(j, _):
        taps = fbuf[pl.ds(pl.multiple_of(j * BLOCK, BLOCK), BLOCK), :]
        kern[j] = dot(tables[:, :BLOCK], taps)
        return 0

    lax.fori_loop(0, TAPS, spectrum, 0)

    get_weight.wait()
    for copy in shares:
        copy.wait_recv()

    def wpiece(dz, dyh, dk=0):
        return wbuf.at[seq_at(dz, dyh, dk)]

    def whalf(dz, dyh, lower):
        return wbuf.at[seq_at(dz, dyh, 0), pl.ds(HALF * lower, HALF)]

    def wsend(ref, device):
        return send(ref, ref, device)

    w_up = wsend(wpiece(0, 0), z_up)
    w_down = wsend(wpiece(0, 0), z_down)
    w_far = wsend(wpiece(0, 0), y_far)
    w_mate = [wsend(wpiece(0, 0), mate)]

    for copy in get_values:
        copy.wait()
    get_backward.wait()
    get_gates.wait()

    def window(q, j):
        old = xbuf[q, lag(j + 1), :]
        new = xbuf[q, lag(j), :]
        old = jnp.where(s >= j + 1, old, jnp.zeros_like(old))
        new = jnp.where(s >= j, new, jnp.zeros_like(new))
        return jnp.concatenate([old, new], axis=0)

    def convolve(q):
        near[q].wait_recv()
        src = (TAPS - 2 * k) * BLOCK
        first = send(xbuf.at[q, pl.ds(pl.multiple_of(src, BLOCK), BLOCK)], xbuf.at[q, lag(1)], mate)
        far[q].wait_recv()
        src = (TAPS - 2 - 2 * k) * BLOCK
        second = send(xbuf.at[q, pl.ds(pl.multiple_of(src, BLOCK), BLOCK)], xbuf.at[q, lag(3)], mate)
        first.wait_recv()
        second.wait_recv()
        for j in range(TAPS):
            zbuf[j] = dot(tables[...], window(q, j))

        def combine(i, _):
            re = pl.ds(pl.multiple_of(i * STRIP, STRIP), STRIP)
            im = pl.ds(pl.multiple_of(i * STRIP + BLOCK, STRIP), STRIP)
            real = jnp.zeros((STRIP, PART), jnp.float32)
            imag = jnp.zeros((STRIP, PART), jnp.float32)
            for j in range(TAPS):
                kr, ki = kern[j, re, cols(q)], kern[j, im, cols(q)]
                wr, wi = zbuf[j, re, :], zbuf[j, im, :]
                real = real + kr * wr - ki * wi
                imag = imag + kr * wi + ki * wr
            ybuf[re, :] = real.astype(jnp.bfloat16)
            ybuf[im, :] = imag.astype(jnp.bfloat16)
            return 0

        lax.fori_loop(0, BLOCK // STRIP, combine, 0)
        now = xbuf[q, lag(0), :].astype(jnp.float32)
        filtered = dot(inverse[...], ybuf[...]) + skip[:, cols(q)] * now
        abuf[c, q] = (gbuf[:, cols(q)].astype(jnp.float32) * filtered).astype(jnp.bfloat16)

    def apiece(q, dyl, dx):
        return abuf.at[chan_at(dyl, dx), q]

    def ahalf(q, dyl, dx, lower):
        return abuf.at[chan_at(dyl, dx), q, pl.ds(HALF * lower, HALF)]

    a_up, a_down, a_near = [], [], []

    def spread(q):
        own = apiece(q, 0, 0)
        a_up.append(send(own, own, x_up))
        a_down.append(send(own, own, x_down))
        a_near.append(send(own, own, y_near))

    a_up2, a_down2, a_nup, a_ndown, a_nfar = [], [], [], [], []

    def relay(q):
        a_up[q].wait_recv()
        ref = ahalf(q, 0, -1, 0)
        a_up2.append(send(ref, ref, x_up))
        a_down[q].wait_recv()
        ref = ahalf(q, 0, 1, 1)
        a_down2.append(send(ref, ref, x_down))
        a_near[q].wait_recv()
        ref = apiece(q, 1, 0)
        a_nup.append(send(ref, ref, x_up))
        a_ndown.append(send(ref, ref, x_down))

    def relay_far(q):
        a_up2[q].wait_recv()
        a_down2[q].wait_recv()
        ref = apiece(q, 0, 2)
        a_nfar.append(send(ref, ref, y_near))

    convolve(0)
    spread(0)
    w_up.wait_recv()
    w_up2 = wsend(whalf(-1, 0, 0), z_up)
    w_mate.append(wsend(wpiece(-1, 0), mate))
    w_down.wait_recv()
    w_down2 = wsend(whalf(1, 0, 1), z_down)
    w_mate.append(wsend(wpiece(1, 0), mate))
    convolve(1)
    spread(1)
    w_far.wait_recv()
    w_fup = wsend(wpiece(0, 1), z_up)
    w_fdown = wsend(wpiece(0, 1), z_down)
    w_mate.append(wsend(wpiece(0, 1), mate))
    relay(0)
    relay(1)
    w_up2.wait_recv()
    w_down2.wait_recv()
    w_mate.append(wsend(wpiece(2, 0), mate))
    relay_far(0)
    relay_far(1)
    w_fup.wait_recv()
    w_fup2 = wsend(whalf(-1, 1, 0), z_up)
    w_mate.append(wsend(wpiece(-1, 1), mate))
    w_fdown.wait_recv()
    w_fdown2 = wsend(whalf(1, 1, 1), z_down)
    w_mate.append(wsend(wpiece(1, 1), mate))
    w_fup2.wait_recv()
    w_fdown2.wait_recv()
    w_mate.append(wsend(wpiece(2, 1), mate))
    for copy in w_mate:
        copy.wait_recv()

    def project(q, dyl, dx, start=False):
        origin = chan_at(dyl, dx)
        row = q * PART
        term = dot(
            abuf[origin, q], wbuf[2 * origin + row // BLOCK, pl.ds(row % BLOCK, PART), :]
        )
        if start:
            acc[...] = term
        else:
            acc[...] += term

    for q in range(CHUNKS):
        project(q, 0, 0, start=q == 0)
        project(q, 0, -1)
        project(q, 0, 1)
        project(q, 1, 0)
        project(q, 0, 2)
    for q in range(CHUNKS):
        a_nup[q].wait_recv()
        project(q, 1, -1)
        a_ndown[q].wait_recv()
        project(q, 1, 1)
        a_nfar[q].wait_recv()
        project(q, 1, 2)

    obuf[...] = acc[...].astype(jnp.bfloat16)
    mine = pltpu.make_async_copy(
        obuf.at[rows_of(c)], out.at[:, wcols(c)], local_sem.at[len(locals_started)]
    )
    mine.start()
    results = []
    for i in range(1, PEERS):
        peer = (c + i) % PEERS
        results.append(send(obuf.at[rows_of(peer)], out.at[:, wcols(c)], chan_dev(peer)))
    mine.wait()
    for copy in results:
        copy.wait_recv()
    for copy in pending:
        copy.wait_send()


MESSAGES = 4 * CHUNKS + 7 + 17 + 8 * CHUNKS + 7


def body(values, gates, filters, skip, out_weight):
    forward, backward = dft_tables(BLOCK)
    forward = jnp.asarray(forward, jnp.bfloat16)
    backward = jnp.asarray(backward, jnp.bfloat16)
    anywhere = pl.BlockSpec(memory_space=pl.ANY)
    local = pl.BlockSpec(memory_space=pltpu.VMEM)
    bf16, f32 = jnp.bfloat16, jnp.float32
    return pl.pallas_call(
        kernel,
        out_shape=jax.ShapeDtypeStruct((ROWS, PEERS * WIDTH), bf16),
        in_specs=[anywhere, anywhere, anywhere, local, anywhere, anywhere, anywhere],
        out_specs=anywhere,
        scratch_shapes=[
            pltpu.VMEM((CHUNKS, (TAPS + 1) * BLOCK, PART), bf16),
            pltpu.VMEM((BLOCK, WIDTH), bf16),
            pltpu.VMEM((TAPS * BLOCK, WIDTH), bf16),
            pltpu.VMEM((2 * BLOCK, 2 * BLOCK), bf16),
            pltpu.VMEM((BLOCK, 2 * BLOCK), bf16),
            pltpu.VMEM((TAPS, 2 * BLOCK, WIDTH), f32),
            pltpu.VMEM((TAPS, 2 * BLOCK, PART), f32),
            pltpu.VMEM((2 * BLOCK, PART), bf16),
            pltpu.VMEM((PEERS, CHUNKS, BLOCK, PART), bf16),
            pltpu.VMEM((GROUPS, BLOCK, WIDTH), bf16),
            pltpu.VMEM((BLOCK, WIDTH), f32),
            pltpu.VMEM((BLOCK, WIDTH), bf16),
            pltpu.SemaphoreType.DMA((MESSAGES,)),
            pltpu.SemaphoreType.DMA((MESSAGES,)),
            pltpu.SemaphoreType.DMA((8,)),
        ],
        compiler_params=pltpu.CompilerParams(
            collective_id=0, has_side_effects=True, vmem_limit_bytes=48 << 20
        ),
    )(values, gates, filters, skip.reshape(1, -1), out_weight, forward, backward)


def solution(mesh):
    in_specs = (
        P("seq", "chan"),
        P("seq", "chan"),
        P(None, "chan"),
        P("chan"),
        P(("seq", "chan"), None),
    )
    out_specs = P(("seq", "chan"), None)
    return jax.shard_map(body, mesh=mesh, in_specs=in_specs, out_specs=out_specs, check_vma=False)
```

```python
import functools

import numpy as np

import jax
import jax.numpy as jnp
from jax import lax
from jax.experimental import pallas as pl
from jax.experimental.pallas import tpu as pltpu
from jax.sharding import PartitionSpec as P

MESH = pl.DeviceIdType.MESH
CHUNKS = 4
BLOCK = 256
WIDTH = 512
PART = WIDTH // CHUNKS
TAPS = 4
PEERS = 8
GROUPS = 16
ROWS = 32
HALF = BLOCK // 2
STRIP = 32
USE_NEAR = True
SCHEDULE = (
    ("f", 0), ("f", 1), ("own",), ("f", 2), ("f", 3), ("cross",),
    ("c", 0), ("s", 0), ("c", 1), ("s", 1), ("wr",), ("c", 2), ("s", 2), ("wo",),
    ("c", 3), ("s", 3), ("r", 0), ("r", 1), ("w2",), ("r", 2), ("R", 0), ("r", 3),
    ("R", 1), ("wro",), ("R", 2), ("R", 3), ("wl",),
)


def dft_tables(block):
    size = 2 * block
    freq = (np.arange(block) + 0.5)[:, None]
    angle = 2.0 * np.pi * freq * np.arange(size)[None, :] / size
    forward = np.concatenate([np.cos(angle), -np.sin(angle)], axis=0)
    late = angle[:, block:]
    backward = np.concatenate([np.cos(late), -np.sin(late)], axis=0).T / block
    return forward, backward


def dot(a, b):
    return jnp.dot(a, b, preferred_element_type=jnp.float32)


def kernel(
    values, gates, filters, skip, weight, forward, backward, out,
    xbuf, gbuf, fbuf, tables, inverse, kern, zbuf, ybuf, abuf, wbuf, acc, obuf,
    send_sem, recv_sem, local_sem,
):
    s = lax.axis_index("seq")
    c = lax.axis_index("chan")
    z, yh, k = s // 4, (s // 2) % 2, s % 2
    yl, x = c // 4, c % 4

    def seq_at(dz, dyh, dk):
        return ((z + dz + 4) % 4) * 4 + ((yh + dyh) % 2) * 2 + (k + dk) % 2

    def chan_at(dyl, dx):
        return ((yl + dyl) % 2) * 4 + (x + dx + 4) % 4

    def seq_dev(index):
        return {"seq": index, "chan": c}

    def chan_dev(index):
        return {"seq": s, "chan": index}

    z_up, z_down = seq_dev(seq_at(1, 0, 0)), seq_dev(seq_at(-1, 0, 0))
    y_far, mate = seq_dev(seq_at(0, 1, 0)), seq_dev(seq_at(0, 0, 1))
    x_up, x_down = chan_dev(chan_at(0, 1)), chan_dev(chan_at(0, -1))
    y_near = chan_dev(chan_at(1, 0))

    pending = []

    def message(src, dst, device):
        index = len(pending)
        copy = pltpu.make_async_remote_copy(
            src_ref=src, dst_ref=dst, send_sem=send_sem.at[index], recv_sem=recv_sem.at[index],
            device_id=device, device_id_type=MESH,
        )
        pending.append(copy)
        return copy

    def send(src, dst, device):
        copy = message(src, dst, device)
        copy.start()
        return copy

    locals_started = []

    def fetch(src, dst):
        copy = pltpu.make_async_copy(src, dst, local_sem.at[len(locals_started)])
        copy.start()
        locals_started.append(copy)
        return copy

    barrier = pltpu.get_barrier_semaphore()
    sources = [chan_dev((c + i) % PEERS) for i in range(1, PEERS)]
    sources += [z_up, z_down, y_far, mate]
    for device in sources:
        pl.semaphore_signal(barrier, inc=1, device_id=device, device_id_type=MESH)

    def cols(q):
        return pl.ds(q * PART, PART)

    def lag(n):
        return pl.ds((TAPS - n) * BLOCK, BLOCK)

    get_filters = fetch(filters, fbuf)
    get_forward = fetch(forward, tables)
    get_values = [fetch(values.at[:, cols(q)], xbuf.at[q, lag(0)]) for q in range(CHUNKS)]
    get_backward = fetch(backward, inverse)
    get_gates = fetch(gates, gbuf)

    def wcols(index):
        return pl.ds(pl.multiple_of(index * WIDTH, WIDTH), WIDTH)

    def rows_of(index):
        return pl.ds(pl.multiple_of(index * ROWS, ROWS), ROWS)

    get_weight = fetch(weight.at[:, wcols(c)], wbuf.at[s, rows_of(c)])

    pl.semaphore_wait(barrier, len(sources))

    far, near, first, second = [], [], [], []
    for q in range(CHUNKS):
        copy = message(values.at[:, cols(q)], xbuf.at[q, lag(4)], z_up)
        pl.when(z < 3)(copy.start)
        far.append(copy)
        src = pl.ds(pl.multiple_of((1 - yh) * TAPS * BLOCK, BLOCK), BLOCK)
        near.append(message(xbuf.at[q, src], xbuf.at[q, lag(2)], y_far))
        src = pl.ds(pl.multiple_of((1 - k) * TAPS * BLOCK, BLOCK), BLOCK)
        dst = pl.ds(pl.multiple_of((3 - 2 * k) * BLOCK, BLOCK), BLOCK)
        first.append(message(xbuf.at[q, src], xbuf.at[q, dst], mate))
        dst = pl.ds(pl.multiple_of((1 + 2 * k) * BLOCK, BLOCK), BLOCK)
        second.append(message(xbuf.at[q, lag(2)], xbuf.at[q, dst], mate))
    shares = []
    for i in range(1, PEERS):
        peer = (c + i) % PEERS
        copy = message(weight.at[:, wcols(peer)], wbuf.at[s, rows_of(c)], chan_dev(peer))
        copy.start()
        shares.append(copy)
    for q in range(CHUNKS):
        get_values[q].wait()
        pl.when(yh == 0)(near[q].start)
        pl.when(k == 0)(first[q].start)

    for n in range(1, TAPS + 1):

        @pl.when(s < n)
        def _():
            for q in range(CHUNKS):
                xbuf[q, lag(n), :] = jnp.zeros((BLOCK, PART), jnp.bfloat16)

    get_filters.wait()
    get_forward.wait()

    def spectrum(j, _):
        taps = fbuf[pl.ds(pl.multiple_of(j * BLOCK, BLOCK), BLOCK), :]
        kern[j] = dot(tables[:, :BLOCK], taps)
        return 0

    lax.fori_loop(0, TAPS, spectrum, 0)
    get_backward.wait()
    get_gates.wait()

    def wpiece(dz, dyh):
        return wbuf.at[seq_at(dz, dyh, 0)]

    def whalf(dz, dyh, lower):
        return wbuf.at[seq_at(dz, dyh, 0), pl.ds(HALF * lower, HALF)]

    w_mate = []

    def to_mate(dz, dyh):
        w_mate.append(send(wpiece(dz, dyh), wpiece(dz, dyh), mate))

    def forward_far(q):
        pl.when(z > 0)(far[q].wait_recv)
        pl.when((yh == 1) & (z > 0))(near[q].start)
        pl.when((k == 1) & (z > 0))(first[q].start)

    def window(q, j):
        return xbuf[q, pl.ds((TAPS - 1 - j) * BLOCK, 2 * BLOCK), :]

    def convolve(q):
        @pl.when(s >= 2)
        def _():
            near[q].wait_recv()
            second[q].start()

        pl.when((k == 1) | (z > 0))(first[q].wait_recv)
        pl.when(s >= 2)(second[q].wait_recv)
        for j in range(TAPS):
            zbuf[j] = dot(tables[...], window(q, j))

        def combine(i, _):
            re = pl.ds(pl.multiple_of(i * STRIP, STRIP), STRIP)
            im = pl.ds(pl.multiple_of(i * STRIP + BLOCK, STRIP), STRIP)
            real = jnp.zeros((STRIP, PART), jnp.float32)
            imag = jnp.zeros((STRIP, PART), jnp.float32)
            for j in range(TAPS):
                kr, ki = kern[j, re, cols(q)], kern[j, im, cols(q)]
                wr, wi = zbuf[j, re, :], zbuf[j, im, :]
                real = real + kr * wr - ki * wi
                imag = imag + kr * wi + ki * wr
            ybuf[re, :] = real.astype(jnp.bfloat16)
            ybuf[im, :] = imag.astype(jnp.bfloat16)
            return 0

        lax.fori_loop(0, BLOCK // STRIP, combine, 0)
        now = xbuf[q, lag(0), :].astype(jnp.float32)
        filtered = dot(inverse[...], ybuf[...]) + skip[:, cols(q)] * now
        abuf[c, :, cols(q)] = (gbuf[:, cols(q)].astype(jnp.float32) * filtered).astype(jnp.bfloat16)

    def apiece(q, dyl, dx):
        return abuf.at[chan_at(dyl, dx), :, cols(q)]

    def ahalf(q, dyl, dx, lower):
        return abuf.at[chan_at(dyl, dx), pl.ds(HALF * lower, HALF), cols(q)]

    def same(ref, device):
        return send(ref, ref, device)

    a_up, a_down, a_near = [], [], []

    def spread(q):
        a_up.append(same(apiece(q, 0, 0), x_up))
        a_down.append(same(apiece(q, 0, 0), x_down))
        a_near.append(same(apiece(q, 0, 0), y_near))

    a_up2, a_down2, a_nup, a_ndown, a_nfar = [], [], [], [], []

    def relay(q):
        a_up[q].wait_recv()
        a_up2.append(same(ahalf(q, 0, -1, 0), x_up))
        a_down[q].wait_recv()
        a_down2.append(same(ahalf(q, 0, 1, 1), x_down))
        a_near[q].wait_recv()
        a_nup.append(same(apiece(q, 1, 0), x_up))
        a_ndown.append(same(apiece(q, 1, 0), x_down))

    def relay_far(q):
        if USE_NEAR:
            a_up2[q].wait_recv()
            a_down2[q].wait_recv()
            a_nfar.append([same(apiece(q, 0, 2), y_near)])
        else:
            a_nup[q].wait_recv()
            up = same(ahalf(q, 1, -1, 0), x_up)
            a_ndown[q].wait_recv()
            a_nfar.append([up, same(ahalf(q, 1, 1, 1), x_down)])

    w = {}

    def w_own():
        get_weight.wait()
        for copy in shares:
            copy.wait_recv()
        w["up"] = same(wpiece(0, 0), z_up)
        w["down"] = same(wpiece(0, 0), z_down)
        to_mate(0, 0)

    def w_cross():
        w["far"] = same(wpiece(0, 0), y_far)

    def w_relay():
        w["down"].wait_recv()
        w["down2"] = same(whalf(1, 0, 1), z_down)
        to_mate(1, 0)
        w["up"].wait_recv()
        w["up2"] = same(whalf(-1, 0, 0), z_up)
        to_mate(-1, 0)

    def w_other():
        w["far"].wait_recv()
        w["fup"] = same(wpiece(0, 1), z_up)
        w["fdown"] = same(wpiece(0, 1), z_down)
        to_mate(0, 1)

    def w_two():
        w["down2"].wait_recv()
        w["up2"].wait_recv()
        to_mate(2, 0)

    def w_relay_other():
        w["fdown"].wait_recv()
        w["fdown2"] = same(whalf(1, 1, 1), z_down)
        to_mate(1, 1)
        w["fup"].wait_recv()
        w["fup2"] = same(whalf(-1, 1, 0), z_up)
        to_mate(-1, 1)

    def w_last():
        w["fdown2"].wait_recv()
        w["fup2"].wait_recv()
        to_mate(2, 1)

    for step in SCHEDULE:
        name, *rest = step
        {
            "f": forward_far, "c": convolve, "s": spread, "r": relay, "R": relay_far,
            "own": w_own, "cross": w_cross, "wr": w_relay, "wo": w_other, "w2": w_two,
            "wro": w_relay_other, "wl": w_last,
        }[name](*rest)
    for copy in w_mate:
        copy.wait_recv()

    def project(dyl, dx, start=False):
        origin = chan_at(dyl, dx)
        term = dot(abuf[origin], wbuf[pl.ds(2 * origin, 2)].reshape(WIDTH, WIDTH))
        if start:
            acc[...] = term
        else:
            acc[...] += term

    project(0, 0, start=True)
    project(0, -1)
    project(0, 1)
    project(1, 0)
    if not USE_NEAR:
        for q in range(CHUNKS):
            a_up2[q].wait_recv()
            a_down2[q].wait_recv()
    project(0, 2)
    if USE_NEAR:
        for q in range(CHUNKS):
            a_nup[q].wait_recv()
            a_ndown[q].wait_recv()
    project(1, -1)
    project(1, 1)
    for group in a_nfar:
        for copy in group:
            copy.wait_recv()
    project(1, 2)

    obuf[...] = acc[...].astype(jnp.bfloat16)
    mine = pltpu.make_async_copy(
        obuf.at[rows_of(c)], out.at[:, wcols(c)], local_sem.at[len(locals_started)]
    )
    mine.start()
    results = []
    for i in range(1, PEERS):
        peer = (c + i) % PEERS
        results.append(send(obuf.at[rows_of(peer)], out.at[:, wcols(c)], chan_dev(peer)))
    mine.wait()
    for copy in results:
        copy.wait_recv()
    for copy in far:
        pl.when(z < 3)(copy.wait_send)
    for copy in near:
        pl.when((yh == 0) | (z > 0))(copy.wait_send)
    for copy in first:
        pl.when((k == 0) | (z > 0))(copy.wait_send)
    for copy in second:
        pl.when(s >= 2)(copy.wait_send)
    for copy in pending:
        if not any(copy is other for other in far + near + first + second):
            copy.wait_send()


MESSAGES = 4 * CHUNKS + 7 + 17 + 9 * CHUNKS + 7


def body(values, gates, filters, skip, out_weight):
    forward, backward = dft_tables(BLOCK)
    forward = jnp.asarray(forward, jnp.bfloat16)
    backward = jnp.asarray(backward, jnp.bfloat16)
    anywhere = pl.BlockSpec(memory_space=pl.ANY)
    local = pl.BlockSpec(memory_space=pltpu.VMEM)
    bf16, f32 = jnp.bfloat16, jnp.float32
    return pl.pallas_call(
        kernel,
        out_shape=jax.ShapeDtypeStruct((ROWS, PEERS * WIDTH), bf16),
        in_specs=[anywhere, anywhere, anywhere, local, anywhere, anywhere, anywhere],
        out_specs=anywhere,
        scratch_shapes=[
            pltpu.VMEM((CHUNKS, (TAPS + 1) * BLOCK, PART), bf16),
            pltpu.VMEM((BLOCK, WIDTH), bf16),
            pltpu.VMEM((TAPS * BLOCK, WIDTH), bf16),
            pltpu.VMEM((2 * BLOCK, 2 * BLOCK), bf16),
            pltpu.VMEM((BLOCK, 2 * BLOCK), bf16),
            pltpu.VMEM((TAPS, 2 * BLOCK, WIDTH), f32),
            pltpu.VMEM((TAPS, 2 * BLOCK, PART), f32),
            pltpu.VMEM((2 * BLOCK, PART), bf16),
            pltpu.VMEM((PEERS, BLOCK, WIDTH), bf16),
            pltpu.VMEM((GROUPS, BLOCK, WIDTH), bf16),
            pltpu.VMEM((BLOCK, WIDTH), f32),
            pltpu.VMEM((BLOCK, WIDTH), bf16),
            pltpu.SemaphoreType.DMA((MESSAGES,)),
            pltpu.SemaphoreType.DMA((MESSAGES,)),
            pltpu.SemaphoreType.DMA((16,)),
        ],
        compiler_params=pltpu.CompilerParams(
            collective_id=0, has_side_effects=True, vmem_limit_bytes=60 * 1024 * 1024
        ),
    )(values, gates, filters, skip.reshape(1, -1), out_weight, forward, backward)


def solution(mesh):
    in_specs = (
        P("seq", "chan"),
        P("seq", "chan"),
        P(None, "chan"),
        P("chan"),
        P(("seq", "chan"), None),
    )
    out_specs = P(("seq", "chan"), None)
    return jax.shard_map(body, mesh=mesh, in_specs=in_specs, out_specs=out_specs, check_vma=False)
```

```python
import functools

import numpy as np

import jax
import jax.numpy as jnp
from jax import lax
from jax.experimental import pallas as pl
from jax.experimental.pallas import tpu as pltpu
from jax.sharding import PartitionSpec as P

MESH = pl.DeviceIdType.MESH
CHUNKS = 4
BLOCK = 256
WIDTH = 512
PART = WIDTH // CHUNKS
TAPS = 4
PEERS = 8
GROUPS = 16
ROWS = 32
HALF = BLOCK // 2
QUARTER = BLOCK // 4
STRIP = 32
USE_NEAR = True
SHARE, RESULT, WEIGHT, GATED, HALO = range(5)
DIRECT = (0,)
SCHEDULE = (
    ("f", 0), ("f", 1), ("n", 0), ("own",), ("x", 0), ("f", 2),
    ("c", 0), ("s", 0), ("f", 3), ("n", 1), ("x", 1), ("c", 1),
    ("s", 1), ("x", 2), ("n", 2), ("r", 0), ("wr",), ("c", 2),
    ("s", 2), ("x", 3), ("n", 3), ("o", 0), ("c", 3), ("s", 3),
    ("r", 1), ("o", 1), ("wm",), ("r", 2), ("o", 2), ("o", 3),
    ("R", 0), ("u", 0), ("u", 1), ("w2",), ("r", 3), ("R", 1),
    ("d", 2), ("R", 2), ("d", 3), ("R", 3), ("wmo",),
)


def dft_tables(block):
    size = 2 * block
    freq = (np.arange(block) + 0.5)[:, None]
    angle = 2.0 * np.pi * freq * np.arange(size)[None, :] / size
    forward = np.concatenate([np.cos(angle), -np.sin(angle)], axis=0)
    late = angle[:, block:]
    backward = np.concatenate([np.cos(late), -np.sin(late)], axis=0).T / block
    return forward, backward


def dot(a, b):
    return jnp.dot(a, b, preferred_element_type=jnp.float32)


def kernel(
    values, gates, filters, skip, weight, forward, backward, out,
    xbuf, gbuf, fbuf, tables, inverse, kern, zbuf, total, ybuf, abuf, wbuf, acc, obuf,
    send_sem, recv_sem, local_sem,
):
    s = lax.axis_index("seq")
    c = lax.axis_index("chan")
    z, yh, k = s // 4, (s // 2) % 2, s % 2
    yl, x = c // 4, c % 4

    def seq_at(dz, dyh, dk):
        return ((z + dz + 4) % 4) * 4 + ((yh + dyh) % 2) * 2 + (k + dk) % 2

    def chan_at(dyl, dx):
        return ((yl + dyl) % 2) * 4 + (x + dx + 4) % 4

    def seq_dev(index):
        return {"seq": index, "chan": c}

    def chan_dev(index):
        return {"seq": s, "chan": index}

    z_up, z_down = seq_dev(seq_at(1, 0, 0)), seq_dev(seq_at(-1, 0, 0))
    y_far, mate = seq_dev(seq_at(0, 1, 0)), seq_dev(seq_at(0, 0, 1))
    x_up, x_down = chan_dev(chan_at(0, 1)), chan_dev(chan_at(0, -1))
    y_near = chan_dev(chan_at(1, 0))

    used = {"send": 4, "recv": 2}

    def take(name):
        used[name] += 1
        return used[name] - 1

    def message(src, dst, device, kind):
        send_index = take("send") if kind == HALO else kind
        recv_index = kind if kind in (SHARE, RESULT) else take("recv")
        return pltpu.make_async_remote_copy(
            src_ref=src, dst_ref=dst, send_sem=send_sem.at[send_index],
            recv_sem=recv_sem.at[recv_index], device_id=device, device_id_type=MESH,
        )

    def send(src, dst, device, kind):
        copy = message(src, dst, device, kind)
        copy.start()
        return copy

    def drain(ref, sem):
        pltpu.make_async_copy(ref, ref, sem).wait()

    locals_started = []

    def fetch(src, dst):
        copy = pltpu.make_async_copy(src, dst, local_sem.at[len(locals_started)])
        copy.start()
        locals_started.append(copy)
        return copy

    barrier = pltpu.get_barrier_semaphore()
    sources = [chan_dev((c + i) % PEERS) for i in range(1, PEERS)]
    sources += [z_up, z_down, y_far, mate, seq_dev((s + GROUPS - 2) % GROUPS)]
    for device in sources:
        pl.semaphore_signal(barrier, inc=1, device_id=device, device_id_type=MESH)

    def cols(q):
        return pl.ds(q * PART, PART)

    def lag(n):
        return pl.ds((TAPS - n) * BLOCK, BLOCK)

    get_filters = fetch(filters, fbuf.at[pl.ds(BLOCK, TAPS * BLOCK)])
    get_forward = fetch(forward, tables)
    get_values = [fetch(values.at[:, cols(q)], xbuf.at[q, lag(0)]) for q in range(CHUNKS)]
    get_backward = fetch(backward, inverse)
    get_gates = fetch(gates, gbuf)

    def wcols(index):
        return pl.ds(pl.multiple_of(index * WIDTH, WIDTH), WIDTH)

    def rows_of(index):
        return pl.ds(pl.multiple_of(index * ROWS, ROWS), ROWS)

    get_weight = fetch(weight.at[:, wcols(c)], wbuf.at[s, rows_of(c)])

    edge = jnp.zeros((BLOCK, WIDTH), jnp.bfloat16)
    fbuf[:BLOCK, :] = edge
    fbuf[(TAPS + 1) * BLOCK :, :] = edge

    pl.semaphore_wait(barrier, len(sources))

    far, near, first, second = [], [], [], []
    for q in range(CHUNKS):
        copy = message(values.at[:, cols(q)], xbuf.at[q, lag(4)], z_up, HALO)
        pl.when(z < 3)(copy.start)
        far.append(copy)
        if q in DIRECT:
            copy = message(values.at[:, cols(q)], xbuf.at[q, lag(2)], seq_dev((s + 2) % GROUPS), HALO)
            pl.when(s + 2 < GROUPS)(copy.start)
        else:
            src = pl.ds(pl.multiple_of((1 - yh) * TAPS * BLOCK, BLOCK), BLOCK)
            copy = message(xbuf.at[q, src], xbuf.at[q, lag(2)], y_far, HALO)
        near.append(copy)
        src = pl.ds(pl.multiple_of((1 - k) * TAPS * BLOCK, BLOCK), BLOCK)
        dst = pl.ds(pl.multiple_of((3 - 2 * k) * BLOCK, BLOCK), BLOCK)
        first.append(message(xbuf.at[q, src], xbuf.at[q, dst], mate, HALO))
        dst = pl.ds(pl.multiple_of((1 + 2 * k) * BLOCK, BLOCK), BLOCK)
        second.append(message(xbuf.at[q, lag(2)], xbuf.at[q, dst], mate, HALO))
    others = [(1, 2), (1, 1), (1, -1), (0, 2), (1, 0), (0, 1), (0, -1)]
    for dyl, dx in others:
        peer = chan_at(dyl, dx)
        send(weight.at[:, wcols(peer)], wbuf.at[s, rows_of(c)], chan_dev(peer), SHARE)
    for q in range(CHUNKS):
        get_values[q].wait()
        if q not in DIRECT:
            pl.when(yh == 0)(near[q].start)
        pl.when(k == 0)(first[q].start)

    for n in range(1, TAPS + 1):

        @pl.when(s < n)
        def _():
            for q in range(CHUNKS):
                xbuf[q, lag(n), :] = jnp.zeros((BLOCK, PART), jnp.bfloat16)

    get_filters.wait()
    get_forward.wait()

    def spectrum(n, _):
        taps = fbuf[pl.ds(pl.multiple_of(n * BLOCK, BLOCK), 2 * BLOCK), :]
        kern[n] = dot(tables[...], taps)
        return 0

    lax.fori_loop(0, TAPS + 1, spectrum, 0)
    for q in range(CHUNKS):
        zbuf[0, :, cols(q)] = dot(tables[:, :BLOCK], xbuf[q, lag(0), :])

    def begin(i, _):
        re = pl.ds(pl.multiple_of(i * STRIP, STRIP), STRIP)
        im = pl.ds(pl.multiple_of(i * STRIP + BLOCK, STRIP), STRIP)
        kr, ki = kern[0, re, :], kern[0, im, :]
        wr, wi = zbuf[0, re, :], zbuf[0, im, :]
        total[re, :] = kr * wr - ki * wi
        total[im, :] = kr * wi + ki * wr
        return 0

    lax.fori_loop(0, BLOCK // STRIP, begin, 0)
    get_backward.wait()
    get_gates.wait()

    def wpiece(dz, dyh):
        return wbuf.at[seq_at(dz, dyh, 0)]

    def whalf(dz, dyh, lower):
        return wbuf.at[seq_at(dz, dyh, 0), pl.ds(HALF * lower, HALF)]

    w_mate = [[], []]

    def to_mate(dz, dyh):
        w_mate[dyh].append(send(wpiece(dz, dyh), wpiece(dz, dyh), mate, WEIGHT))

    def forward_far(q):
        pl.when(z > 0)(far[q].wait_recv)
        if q not in DIRECT:
            pl.when((yh == 1) & (z > 0))(near[q].start)
        pl.when((k == 1) & (z > 0))(first[q].start)

    def mates(q):
        @pl.when(s >= 2)
        def _():
            near[q].wait_recv()
            second[q].start()

    def convolve(q):
        pl.when((k == 1) | (z > 0))(first[q].wait_recv)
        pl.when(s >= 2)(second[q].wait_recv)
        for n in range(1, TAPS + 1):
            zbuf[n, :, cols(q)] = dot(tables[:, :BLOCK], xbuf[q, lag(n), :])

        def combine(i, _):
            re = pl.ds(pl.multiple_of(i * STRIP, STRIP), STRIP)
            im = pl.ds(pl.multiple_of(i * STRIP + BLOCK, STRIP), STRIP)
            real, imag = total[re, cols(q)], total[im, cols(q)]
            for n in range(1, TAPS + 1):
                kr, ki = kern[n, re, cols(q)], kern[n, im, cols(q)]
                wr, wi = zbuf[n, re, cols(q)], zbuf[n, im, cols(q)]
                real = real + kr * wr - ki * wi
                imag = imag + kr * wi + ki * wr
            ybuf[re, :] = real.astype(jnp.bfloat16)
            ybuf[im, :] = imag.astype(jnp.bfloat16)
            return 0

        lax.fori_loop(0, BLOCK // STRIP, combine, 0)
        now = xbuf[q, lag(0), :].astype(jnp.float32)
        filtered = dot(inverse[...], ybuf[...]) + skip[:, cols(q)] * now
        abuf[c, :, cols(q)] = (gbuf[:, cols(q)].astype(jnp.float32) * filtered).astype(jnp.bfloat16)

    def apiece(q, dyl, dx):
        return abuf.at[chan_at(dyl, dx), :, cols(q)]

    def ahalf(q, dyl, dx, lower):
        return abuf.at[chan_at(dyl, dx), pl.ds(HALF * lower, HALF), cols(q)]

    def same(ref, device, kind=WEIGHT):
        return send(ref, ref, device, kind)

    def gate(ref, device):
        return send(ref, ref, device, GATED)

    a_up, a_down, a_near = [], [], []

    def spread(q):
        a_up.append(gate(apiece(q, 0, 0), x_up))
        a_down.append(gate(apiece(q, 0, 0), x_down))
        a_near.append(gate(apiece(q, 0, 0), y_near))

    a_up2, a_down2, a_nup, a_ndown, a_nfar = [], [], [], [], []

    def relay(q):
        a_up[q].wait_recv()
        a_up2.append(gate(ahalf(q, 0, -1, 0), x_up))
        a_down[q].wait_recv()
        a_down2.append(gate(ahalf(q, 0, 1, 1), x_down))
        a_near[q].wait_recv()
        a_nup.append(gate(apiece(q, 1, 0), x_up))
        a_ndown.append(gate(apiece(q, 1, 0), x_down))

    def relay_far(q):
        if USE_NEAR:
            a_up2[q].wait_recv()
            a_down2[q].wait_recv()
            a_nfar.append([gate(apiece(q, 0, 2), y_near)])
        else:
            a_nup[q].wait_recv()
            up = gate(ahalf(q, 1, -1, 0), x_up)
            a_ndown[q].wait_recv()
            a_nfar.append([up, gate(ahalf(q, 1, 1, 1), x_down)])

    w = {}

    def both(dz, dyh, device, order):
        return [same(whalf(dz, dyh, lower), device) for lower in order]

    def ready(name):
        for copy in w[name]:
            copy.wait_recv()

    def w_own():
        get_weight.wait()
        drain(wbuf.at[0, pl.ds(0, BLOCK - ROWS)], recv_sem.at[SHARE])
        w["up"] = both(0, 0, z_up, (0, 1))
        w["down"] = both(0, 0, z_down, (1, 0))
        to_mate(0, 0)

    def wquarter(i):
        return wbuf.at[seq_at(0, 0, 0), pl.ds(i * QUARTER, QUARTER)]

    def wother(i):
        return wbuf.at[seq_at(0, 1, 0), pl.ds(i * QUARTER, QUARTER)]

    w["far"], w["fup"], w["fdown"] = [], [], []

    def w_cross(i):
        w["far"].append(same(wquarter(i), y_far))

    def w_relay():
        w["down"].pop(0).wait_recv()
        w["down2"] = same(whalf(1, 0, 1), z_down)
        w["up"].pop(0).wait_recv()
        w["up2"] = same(whalf(-1, 0, 0), z_up)

    def w_mates():
        ready("down")
        to_mate(1, 0)
        ready("up")
        to_mate(-1, 0)

    def w_other(i):
        w["far"][i].wait_recv()
        w["fup"].append(same(wother(i), z_up))
        w["fdown"].append(same(wother(i), z_down))
        if i == 3:
            to_mate(0, 1)

    def w_two():
        w["down2"].wait_recv()
        w["up2"].wait_recv()
        to_mate(2, 0)

    def wnext(dz, i):
        return wbuf.at[seq_at(dz, 1, 0), pl.ds(i * QUARTER, QUARTER)]

    w["fup2"], w["fdown2"] = [], []

    def w_relay_up(i):
        w["fup"][i].wait_recv()
        w["fup2"].append(same(wnext(-1, i), z_up))

    def w_relay_down(i):
        w["fdown"][i].wait_recv()
        w["fdown2"].append(same(wnext(1, i), z_down))

    def w_mates_other():
        for copy in w["fdown"][:2]:
            copy.wait_recv()
        to_mate(1, 1)
        for copy in w["fup"][2:]:
            copy.wait_recv()
        to_mate(-1, 1)

    def w_last():
        for copy in w["fup2"]:
            copy.wait_recv()
        last = [same(whalf(2, 1, 0), mate)]
        for copy in w["fdown2"]:
            copy.wait_recv()
        last.append(same(whalf(2, 1, 1), mate))
        for copy in last:
            copy.wait_recv()

    for step in SCHEDULE:
        name, *rest = step
        {
            "f": forward_far, "n": mates, "c": convolve, "s": spread, "r": relay, "R": relay_far,
            "own": w_own, "x": w_cross, "wr": w_relay, "o": w_other, "w2": w_two,
            "u": w_relay_up, "d": w_relay_down, "wm": w_mates, "wmo": w_mates_other,
        }[name](*rest)
    def project(origin):
        acc[...] += dot(abuf[origin], wbuf[pl.ds(2 * origin, 2)].reshape(WIDTH, WIDTH))

    assert used["send"] <= SENDS and used["recv"] <= ARRIVALS, used
    acc[...] = jnp.zeros_like(acc)
    last_a = chan_at(1, 2)
    last_w = seq_at(2, 1, 0) // 2

    def group(first):
        for step in (0, 2):
            origin = first + step
            pl.when((origin != last_a) & (origin != last_w))(functools.partial(project, origin))

    def wait_all(copies):
        for copy in copies:
            copy.wait_recv()

    wait_all(w_mate[0])
    group(4 * yl + yh)
    wait_all(w_mate[1])
    group(4 * yl + 1 - yh)
    wait_all(a_nup + a_ndown)
    group(4 * (1 - yl) + yh)
    group(4 * (1 - yl) + 1 - yh)
    for copies in a_nfar:
        wait_all(copies)
    pl.when(last_a != last_w)(functools.partial(project, last_a))
    w_last()
    project(last_w)
    obuf[...] = acc[...].astype(jnp.bfloat16)
    mine = pltpu.make_async_copy(
        obuf.at[rows_of(c)], out.at[:, wcols(c)], local_sem.at[len(locals_started)]
    )
    mine.start()
    for dyl, dx in others:
        peer = chan_at(dyl, dx)
        send(obuf.at[rows_of(peer)], out.at[:, wcols(c)], chan_dev(peer), RESULT)
    for copy in far:
        pl.when(z < 3)(copy.wait_send)
    for q, copy in enumerate(near):
        started = s + 2 < GROUPS if q in DIRECT else (yh == 0) | (z > 0)
        pl.when(started)(copy.wait_send)
    for copy in first:
        pl.when((k == 0) | (z > 0))(copy.wait_send)
    for copy in second:
        pl.when(s >= 2)(copy.wait_send)
    part = wbuf.at[0, pl.ds(0, BLOCK - ROWS)]
    drain(part, send_sem.at[SHARE])
    drain(wbuf.at[pl.ds(0, 15)], send_sem.at[WEIGHT])
    drain(wbuf.at[pl.ds(0, 7)], send_sem.at[GATED])
    drain(part, send_sem.at[RESULT])
    mine.wait()
    drain(part, recv_sem.at[RESULT])


SENDS = 4 + 4 * CHUNKS
ARRIVALS = 2 + 4 * CHUNKS + 32 + 9 * CHUNKS


def body(values, gates, filters, skip, out_weight):
    forward, backward = dft_tables(BLOCK)
    forward = jnp.asarray(forward, jnp.bfloat16)
    backward = jnp.asarray(backward, jnp.bfloat16)
    anywhere = pl.BlockSpec(memory_space=pl.ANY)
    local = pl.BlockSpec(memory_space=pltpu.VMEM)
    bf16, f32 = jnp.bfloat16, jnp.float32
    return pl.pallas_call(
        kernel,
        out_shape=jax.ShapeDtypeStruct((ROWS, PEERS * WIDTH), bf16),
        in_specs=[anywhere, anywhere, anywhere, local, anywhere, anywhere, anywhere],
        out_specs=anywhere,
        scratch_shapes=[
            pltpu.VMEM((CHUNKS, (TAPS + 1) * BLOCK, PART), bf16),
            pltpu.VMEM((BLOCK, WIDTH), bf16),
            pltpu.VMEM(((TAPS + 2) * BLOCK, WIDTH), bf16),
            pltpu.VMEM((2 * BLOCK, 2 * BLOCK), bf16),
            pltpu.VMEM((BLOCK, 2 * BLOCK), bf16),
            pltpu.VMEM((TAPS + 1, 2 * BLOCK, WIDTH), f32),
            pltpu.VMEM((TAPS + 1, 2 * BLOCK, WIDTH), f32),
            pltpu.VMEM((2 * BLOCK, WIDTH), f32),
            pltpu.VMEM((2 * BLOCK, PART), bf16),
            pltpu.VMEM((PEERS, BLOCK, WIDTH), bf16),
            pltpu.VMEM((GROUPS, BLOCK, WIDTH), bf16),
            pltpu.VMEM((BLOCK, WIDTH), f32),
            pltpu.VMEM((BLOCK, WIDTH), bf16),
            pltpu.SemaphoreType.DMA((SENDS,)),
            pltpu.SemaphoreType.DMA((ARRIVALS,)),
            pltpu.SemaphoreType.DMA((10,)),
        ],
        compiler_params=pltpu.CompilerParams(
            collective_id=0, has_side_effects=True, vmem_limit_bytes=60 * 1024 * 1024
        ),
    )(values, gates, filters, skip.reshape(1, -1), out_weight, forward, backward)


def solution(mesh):
    in_specs = (
        P("seq", "chan"),
        P("seq", "chan"),
        P(None, "chan"),
        P("chan"),
        P(("seq", "chan"), None),
    )
    out_specs = P(("seq", "chan"), None)
    return jax.shard_map(body, mesh=mesh, in_specs=in_specs, out_specs=out_specs, check_vma=False)
```

```python
import functools

import numpy as np

import jax
import jax.numpy as jnp
from jax import lax
from jax.experimental import pallas as pl
from jax.experimental.pallas import tpu as pltpu
from jax.sharding import PartitionSpec as P

MESH = pl.DeviceIdType.MESH
CHUNKS = 4
BLOCK = 256
WIDTH = 512
PART = WIDTH // CHUNKS
TAPS = 4
PEERS = 8
GROUPS = 16
ROWS = 32
HALF = BLOCK // 2
QUARTER = BLOCK // 4
STRIP = 32
USE_NEAR = True
SHARE, RESULT, WEIGHT, GATED, HALO = range(5)
DIRECT = (0,)
SCHEDULE = (
    ("f", 0), ("f", 1), ("n", 0), ("own",), ("x", 0), ("f", 2),
    ("c", 0), ("s", 0), ("x", 1), ("f", 3), ("n", 1), ("x", 2),
    ("c", 1), ("s", 1), ("x", 3), ("n", 2), ("r", 0), ("wr",),
    ("o", 0), ("c", 2), ("s", 2), ("n", 3), ("o", 1), ("c", 3),
    ("s", 3), ("r", 1), ("wm",), ("o", 2), ("r", 2), ("o", 3),
    ("u", 0), ("R", 0), ("u", 1), ("w2",), ("d", 2), ("r", 3),
    ("R", 1), ("R", 2), ("d", 3), ("R", 3), ("wmo",),
)


def dft_tables(block):
    size = 2 * block
    freq = (np.arange(block) + 0.5)[:, None]
    angle = 2.0 * np.pi * freq * np.arange(size)[None, :] / size
    forward = np.concatenate([np.cos(angle), -np.sin(angle)], axis=0)
    late = angle[:, block:]
    backward = np.concatenate([np.cos(late), -np.sin(late)], axis=0).T / block
    return forward, backward


def dot(a, b):
    return jnp.dot(a, b, preferred_element_type=jnp.float32)


def kernel(
    values, gates, filters, skip, weight, forward, backward, out,
    xbuf, gbuf, fbuf, tables, inverse, kern, zbuf, total, ybuf, abuf, wbuf, acc, obuf,
    send_sem, recv_sem, local_sem,
):
    s = lax.axis_index("seq")
    c = lax.axis_index("chan")
    z, yh, k = s // 4, (s // 2) % 2, s % 2
    yl, x = c // 4, c % 4

    def seq_at(dz, dyh, dk):
        return ((z + dz + 4) % 4) * 4 + ((yh + dyh) % 2) * 2 + (k + dk) % 2

    def chan_at(dyl, dx):
        return ((yl + dyl) % 2) * 4 + (x + dx + 4) % 4

    def seq_dev(index):
        return {"seq": index, "chan": c}

    def chan_dev(index):
        return {"seq": s, "chan": index}

    z_up, z_down = seq_dev(seq_at(1, 0, 0)), seq_dev(seq_at(-1, 0, 0))
    y_far, mate = seq_dev(seq_at(0, 1, 0)), seq_dev(seq_at(0, 0, 1))
    x_up, x_down = chan_dev(chan_at(0, 1)), chan_dev(chan_at(0, -1))
    y_near = chan_dev(chan_at(1, 0))

    used = {"send": 4, "recv": 2}

    def take(name):
        used[name] += 1
        return used[name] - 1

    def message(src, dst, device, kind):
        send_index = take("send") if kind == HALO else kind
        recv_index = kind if kind in (SHARE, RESULT) else take("recv")
        return pltpu.make_async_remote_copy(
            src_ref=src, dst_ref=dst, send_sem=send_sem.at[send_index],
            recv_sem=recv_sem.at[recv_index], device_id=device, device_id_type=MESH,
        )

    def send(src, dst, device, kind):
        copy = message(src, dst, device, kind)
        copy.start()
        return copy

    def drain(ref, sem):
        pltpu.make_async_copy(ref, ref, sem).wait()

    locals_started = []

    def fetch(src, dst):
        copy = pltpu.make_async_copy(src, dst, local_sem.at[len(locals_started)])
        copy.start()
        locals_started.append(copy)
        return copy

    barrier = pltpu.get_barrier_semaphore()
    sources = [chan_dev((c + i) % PEERS) for i in range(1, PEERS)]
    sources += [z_up, z_down, y_far, mate, seq_dev((s + GROUPS - 2) % GROUPS)]
    for device in sources:
        pl.semaphore_signal(barrier, inc=1, device_id=device, device_id_type=MESH)

    def cols(q):
        return pl.ds(q * PART, PART)

    def lag(n):
        return pl.ds((TAPS - n) * BLOCK, BLOCK)

    get_filters = fetch(filters, fbuf.at[pl.ds(BLOCK, TAPS * BLOCK)])
    get_forward = fetch(forward, tables)
    get_values = [fetch(values.at[:, cols(q)], xbuf.at[q, lag(0)]) for q in range(CHUNKS)]
    get_backward = fetch(backward, inverse)
    get_gates = fetch(gates, gbuf)

    def wcols(index):
        return pl.ds(pl.multiple_of(index * WIDTH, WIDTH), WIDTH)

    def rows_of(index):
        return pl.ds(pl.multiple_of(index * ROWS, ROWS), ROWS)

    get_weight = fetch(weight.at[:, wcols(c)], wbuf.at[s, rows_of(c)])

    edge = jnp.zeros((BLOCK, WIDTH), jnp.bfloat16)
    fbuf[:BLOCK, :] = edge
    fbuf[(TAPS + 1) * BLOCK :, :] = edge

    pl.semaphore_wait(barrier, len(sources))

    far, near, first, second = [], [], [], []
    straight = {}
    for q in DIRECT:
        straight[q] = message(values.at[:, cols(q)], xbuf.at[q, lag(2)], seq_dev((s + 2) % GROUPS), HALO)
        pl.when(s + 2 < GROUPS)(straight[q].start)
    for q in range(CHUNKS):
        copy = message(values.at[:, cols(q)], xbuf.at[q, lag(4)], z_up, HALO)
        pl.when(z < 3)(copy.start)
        far.append(copy)
        if q in DIRECT:
            copy = straight[q]
        else:
            src = pl.ds(pl.multiple_of((1 - yh) * TAPS * BLOCK, BLOCK), BLOCK)
            copy = message(xbuf.at[q, src], xbuf.at[q, lag(2)], y_far, HALO)
        near.append(copy)
        src = pl.ds(pl.multiple_of((1 - k) * TAPS * BLOCK, BLOCK), BLOCK)
        dst = pl.ds(pl.multiple_of((3 - 2 * k) * BLOCK, BLOCK), BLOCK)
        first.append(message(xbuf.at[q, src], xbuf.at[q, dst], mate, HALO))
        dst = pl.ds(pl.multiple_of((1 + 2 * k) * BLOCK, BLOCK), BLOCK)
        second.append(message(xbuf.at[q, lag(2)], xbuf.at[q, dst], mate, HALO))
    others = [(1, 2), (1, 1), (1, -1), (0, 2), (1, 0), (0, 1), (0, -1)]
    for dyl, dx in others:
        peer = chan_at(dyl, dx)
        send(weight.at[:, wcols(peer)], wbuf.at[s, rows_of(c)], chan_dev(peer), SHARE)
    for q in range(CHUNKS):
        get_values[q].wait()
        if q not in DIRECT:
            pl.when(yh == 0)(near[q].start)
        pl.when(k == 0)(first[q].start)

    for n in range(1, TAPS + 1):

        @pl.when(s < n)
        def _():
            for q in range(CHUNKS):
                xbuf[q, lag(n), :] = jnp.zeros((BLOCK, PART), jnp.bfloat16)

    get_filters.wait()
    get_forward.wait()

    def spectrum(n, _):
        taps = fbuf[pl.ds(pl.multiple_of(n * BLOCK, BLOCK), 2 * BLOCK), :]
        kern[n] = dot(tables[...], taps)
        return 0

    lax.fori_loop(0, TAPS + 1, spectrum, 0)
    for q in range(CHUNKS):
        zbuf[0, :, cols(q)] = dot(tables[:, :BLOCK], xbuf[q, lag(0), :])

    def begin(i, _):
        re = pl.ds(pl.multiple_of(i * STRIP, STRIP), STRIP)
        im = pl.ds(pl.multiple_of(i * STRIP + BLOCK, STRIP), STRIP)
        kr, ki = kern[0, re, :], kern[0, im, :]
        wr, wi = zbuf[0, re, :], zbuf[0, im, :]
        total[re, :] = kr * wr - ki * wi
        total[im, :] = kr * wi + ki * wr
        return 0

    lax.fori_loop(0, BLOCK // STRIP, begin, 0)
    get_backward.wait()
    get_gates.wait()

    def wpiece(dz, dyh):
        return wbuf.at[seq_at(dz, dyh, 0)]

    def whalf(dz, dyh, lower):
        return wbuf.at[seq_at(dz, dyh, 0), pl.ds(HALF * lower, HALF)]

    w_mate = [[], []]

    def to_mate(dz, dyh):
        w_mate[dyh].append(send(wpiece(dz, dyh), wpiece(dz, dyh), mate, WEIGHT))

    def forward_far(q):
        pl.when(z > 0)(far[q].wait_recv)
        if q not in DIRECT:
            pl.when((yh == 1) & (z > 0))(near[q].start)
        pl.when((k == 1) & (z > 0))(first[q].start)

    def mates(q):
        @pl.when(s >= 2)
        def _():
            near[q].wait_recv()
            second[q].start()

    def convolve(q):
        pl.when((k == 1) | (z > 0))(first[q].wait_recv)
        pl.when(s >= 2)(second[q].wait_recv)
        for n in range(1, TAPS + 1):
            zbuf[n, :, cols(q)] = dot(tables[:, :BLOCK], xbuf[q, lag(n), :])

        def combine(i, _):
            re = pl.ds(pl.multiple_of(i * STRIP, STRIP), STRIP)
            im = pl.ds(pl.multiple_of(i * STRIP + BLOCK, STRIP), STRIP)
            real, imag = total[re, cols(q)], total[im, cols(q)]
            for n in range(1, TAPS + 1):
                kr, ki = kern[n, re, cols(q)], kern[n, im, cols(q)]
                wr, wi = zbuf[n, re, cols(q)], zbuf[n, im, cols(q)]
                real = real + kr * wr - ki * wi
                imag = imag + kr * wi + ki * wr
            ybuf[re, :] = real.astype(jnp.bfloat16)
            ybuf[im, :] = imag.astype(jnp.bfloat16)
            return 0

        lax.fori_loop(0, BLOCK // STRIP, combine, 0)
        now = xbuf[q, lag(0), :].astype(jnp.float32)
        filtered = dot(inverse[...], ybuf[...]) + skip[:, cols(q)] * now
        abuf[c, :, cols(q)] = (gbuf[:, cols(q)].astype(jnp.float32) * filtered).astype(jnp.bfloat16)

    def apiece(q, dyl, dx):
        return abuf.at[chan_at(dyl, dx), :, cols(q)]

    def ahalf(q, dyl, dx, lower):
        return abuf.at[chan_at(dyl, dx), pl.ds(HALF * lower, HALF), cols(q)]

    def same(ref, device, kind=WEIGHT):
        return send(ref, ref, device, kind)

    def gate(ref, device):
        return send(ref, ref, device, GATED)

    a_up, a_down, a_near = [], [], []

    def spread(q):
        a_up.append(gate(apiece(q, 0, 0), x_up))
        a_down.append(gate(apiece(q, 0, 0), x_down))
        a_near.append(gate(apiece(q, 0, 0), y_near))

    a_up2, a_down2, a_nup, a_ndown, a_nfar = [], [], [], [], []

    def relay(q):
        a_up[q].wait_recv()
        a_up2.append(gate(ahalf(q, 0, -1, 0), x_up))
        a_down[q].wait_recv()
        a_down2.append(gate(ahalf(q, 0, 1, 1), x_down))
        a_near[q].wait_recv()
        a_nup.append(gate(apiece(q, 1, 0), x_up))
        a_ndown.append(gate(apiece(q, 1, 0), x_down))

    def relay_far(q):
        if USE_NEAR:
            a_up2[q].wait_recv()
            a_down2[q].wait_recv()
            a_nfar.append([gate(apiece(q, 0, 2), y_near)])
        else:
            a_nup[q].wait_recv()
            up = gate(ahalf(q, 1, -1, 0), x_up)
            a_ndown[q].wait_recv()
            a_nfar.append([up, gate(ahalf(q, 1, 1, 1), x_down)])

    w = {}

    def both(dz, dyh, device, order):
        return [same(whalf(dz, dyh, lower), device) for lower in order]

    def ready(name):
        for copy in w[name]:
            copy.wait_recv()

    def w_own():
        get_weight.wait()
        drain(wbuf.at[0, pl.ds(0, BLOCK - ROWS)], recv_sem.at[SHARE])
        w["up"] = both(0, 0, z_up, (0, 1))
        w["down"] = both(0, 0, z_down, (1, 0))
        to_mate(0, 0)

    def wquarter(i):
        return wbuf.at[seq_at(0, 0, 0), pl.ds(i * QUARTER, QUARTER)]

    def wother(i):
        return wbuf.at[seq_at(0, 1, 0), pl.ds(i * QUARTER, QUARTER)]

    w["far"], w["fup"], w["fdown"] = [], [], []

    def w_cross(i):
        w["far"].append(same(wquarter(i), y_far))

    def w_relay():
        w["down"].pop(0).wait_recv()
        w["down2"] = same(whalf(1, 0, 1), z_down)
        w["up"].pop(0).wait_recv()
        w["up2"] = same(whalf(-1, 0, 0), z_up)

    def w_mates():
        ready("down")
        to_mate(1, 0)
        ready("up")
        to_mate(-1, 0)

    def w_other(i):
        w["far"][i].wait_recv()
        w["fup"].append(same(wother(i), z_up))
        w["fdown"].append(same(wother(i), z_down))
        if i == 3:
            to_mate(0, 1)

    def w_two():
        w["down2"].wait_recv()
        w["up2"].wait_recv()
        to_mate(2, 0)

    def wnext(dz, i):
        return wbuf.at[seq_at(dz, 1, 0), pl.ds(i * QUARTER, QUARTER)]

    w["fup2"], w["fdown2"] = [], []

    def w_relay_up(i):
        w["fup"][i].wait_recv()
        w["fup2"].append(same(wnext(-1, i), z_up))

    def w_relay_down(i):
        w["fdown"][i].wait_recv()
        w["fdown2"].append(same(wnext(1, i), z_down))

    def w_mates_other():
        for copy in w["fdown"][:2]:
            copy.wait_recv()
        to_mate(1, 1)
        for copy in w["fup"][2:]:
            copy.wait_recv()
        to_mate(-1, 1)

    def w_last():
        for copy in w["fup2"]:
            copy.wait_recv()
        last = [same(whalf(2, 1, 0), mate)]
        for copy in w["fdown2"]:
            copy.wait_recv()
        last.append(same(whalf(2, 1, 1), mate))
        return last

    for step in SCHEDULE:
        name, *rest = step
        {
            "f": forward_far, "n": mates, "c": convolve, "s": spread, "r": relay, "R": relay_far,
            "own": w_own, "x": w_cross, "wr": w_relay, "o": w_other, "w2": w_two,
            "u": w_relay_up, "d": w_relay_down, "wm": w_mates, "wmo": w_mates_other,
        }[name](*rest)
    def project(origin):
        acc[...] += dot(abuf[origin], wbuf[pl.ds(2 * origin, 2)].reshape(WIDTH, WIDTH))

    assert used["send"] <= SENDS and used["recv"] <= ARRIVALS, used
    acc[...] = jnp.zeros_like(acc)
    last_a = chan_at(1, 2)
    last_w = seq_at(2, 1, 0) // 2

    def group(first):
        for step in (0, 2):
            origin = first + step
            pl.when((origin != last_a) & (origin != last_w))(functools.partial(project, origin))

    def wait_all(copies):
        for copy in copies:
            copy.wait_recv()

    wait_all(w_mate[0])
    group(4 * yl + yh)
    final = w_last()
    wait_all(w_mate[1])
    group(4 * yl + 1 - yh)
    wait_all(a_nup + a_ndown)
    group(4 * (1 - yl) + yh)
    group(4 * (1 - yl) + 1 - yh)
    for copies in a_nfar:
        wait_all(copies)
    pl.when(last_a != last_w)(functools.partial(project, last_a))
    wait_all(final)
    project(last_w)
    obuf[...] = acc[...].astype(jnp.bfloat16)
    mine = pltpu.make_async_copy(
        obuf.at[rows_of(c)], out.at[:, wcols(c)], local_sem.at[len(locals_started)]
    )
    mine.start()
    for dyl, dx in others:
        peer = chan_at(dyl, dx)
        send(obuf.at[rows_of(peer)], out.at[:, wcols(c)], chan_dev(peer), RESULT)
    for copy in far:
        pl.when(z < 3)(copy.wait_send)
    for q, copy in enumerate(near):
        started = s + 2 < GROUPS if q in DIRECT else (yh == 0) | (z > 0)
        pl.when(started)(copy.wait_send)
    for copy in first:
        pl.when((k == 0) | (z > 0))(copy.wait_send)
    for copy in second:
        pl.when(s >= 2)(copy.wait_send)
    part = wbuf.at[0, pl.ds(0, BLOCK - ROWS)]
    drain(part, send_sem.at[SHARE])
    drain(wbuf.at[pl.ds(0, 15)], send_sem.at[WEIGHT])
    drain(wbuf.at[pl.ds(0, 7)], send_sem.at[GATED])
    drain(part, send_sem.at[RESULT])
    mine.wait()
    drain(part, recv_sem.at[RESULT])


SENDS = 4 + 4 * CHUNKS
ARRIVALS = 2 + 4 * CHUNKS + 32 + 9 * CHUNKS


def body(values, gates, filters, skip, out_weight):
    forward, backward = dft_tables(BLOCK)
    forward = jnp.asarray(forward, jnp.bfloat16)
    backward = jnp.asarray(backward, jnp.bfloat16)
    anywhere = pl.BlockSpec(memory_space=pl.ANY)
    local = pl.BlockSpec(memory_space=pltpu.VMEM)
    bf16, f32 = jnp.bfloat16, jnp.float32
    return pl.pallas_call(
        kernel,
        out_shape=jax.ShapeDtypeStruct((ROWS, PEERS * WIDTH), bf16),
        in_specs=[anywhere, anywhere, anywhere, local, anywhere, anywhere, anywhere],
        out_specs=anywhere,
        scratch_shapes=[
            pltpu.VMEM((CHUNKS, (TAPS + 1) * BLOCK, PART), bf16),
            pltpu.VMEM((BLOCK, WIDTH), bf16),
            pltpu.VMEM(((TAPS + 2) * BLOCK, WIDTH), bf16),
            pltpu.VMEM((2 * BLOCK, 2 * BLOCK), bf16),
            pltpu.VMEM((BLOCK, 2 * BLOCK), bf16),
            pltpu.VMEM((TAPS + 1, 2 * BLOCK, WIDTH), f32),
            pltpu.VMEM((TAPS + 1, 2 * BLOCK, WIDTH), f32),
            pltpu.VMEM((2 * BLOCK, WIDTH), f32),
            pltpu.VMEM((2 * BLOCK, PART), bf16),
            pltpu.VMEM((PEERS, BLOCK, WIDTH), bf16),
            pltpu.VMEM((GROUPS, BLOCK, WIDTH), bf16),
            pltpu.VMEM((BLOCK, WIDTH), f32),
            pltpu.VMEM((BLOCK, WIDTH), bf16),
            pltpu.SemaphoreType.DMA((SENDS,)),
            pltpu.SemaphoreType.DMA((ARRIVALS,)),
            pltpu.SemaphoreType.DMA((10,)),
        ],
        compiler_params=pltpu.CompilerParams(
            collective_id=0, has_side_effects=True, vmem_limit_bytes=60 * 1024 * 1024
        ),
    )(values, gates, filters, skip.reshape(1, -1), out_weight, forward, backward)


def solution(mesh):
    in_specs = (
        P("seq", "chan"),
        P("seq", "chan"),
        P(None, "chan"),
        P("chan"),
        P(("seq", "chan"), None),
    )
    out_specs = P(("seq", "chan"), None)
    return jax.shard_map(body, mesh=mesh, in_specs=in_specs, out_specs=out_specs, check_vma=False)
```

```python
import functools

import numpy as np

import jax
import jax.numpy as jnp
from jax import lax
from jax.experimental import pallas as pl
from jax.experimental.pallas import tpu as pltpu
from jax.sharding import PartitionSpec as P

MESH = pl.DeviceIdType.MESH
CHUNKS = 4
BLOCK = 256
WIDTH = 512
PART = WIDTH // CHUNKS
TAPS = 4
PEERS = 8
GROUPS = 16
ROWS = 32
HALF = BLOCK // 2
QUARTER = BLOCK // 4
STRIP = 32
SHARE, RESULT, WEIGHT, GATED, FAR, FIRST, SECOND, NEAR, STRAIGHT = range(9)
RELAYED, ACROSS, MATES = 2, 3, 4
DIRECT = (0,)
SCHEDULE = (
    ("f", 0), ("f", 1), ("n", 0), ("own",), ("x", 0), ("f", 2),
    ("c", 0), ("s", 0), ("x", 1), ("f", 3), ("n", 1), ("x", 2),
    ("c", 1), ("s", 1), ("x", 3), ("n", 2), ("r", 0), ("wr",),
    ("o", 0), ("c", 2), ("s", 2), ("n", 3), ("o", 1), ("c", 3),
    ("s", 3), ("r", 1), ("wm",), ("o", 2), ("r", 2), ("o", 3),
    ("u", 0), ("R", 0), ("u", 1), ("w2",), ("d", 2), ("r", 3),
    ("R", 1), ("R", 2), ("d", 3), ("R", 3), ("wmo",),
)


def dft_tables(block):
    size = 2 * block
    freq = (np.arange(block) + 0.5)[:, None]
    angle = 2.0 * np.pi * freq * np.arange(size)[None, :] / size
    forward = np.concatenate([np.cos(angle), -np.sin(angle)], axis=0)
    late = angle[:, block:]
    backward = np.concatenate([np.cos(late), -np.sin(late)], axis=0).T / block
    return forward, backward


def dot(a, b):
    return jnp.dot(a, b, preferred_element_type=jnp.float32)


def kernel(
    values, gates, filters, skip, weight, forward, backward, out,
    xbuf, gbuf, fbuf, tables, inverse, kern, zbuf, total, ybuf, abuf, wbuf, acc, obuf,
    send_sem, recv_sem, local_sem,
):
    s = lax.axis_index("seq")
    c = lax.axis_index("chan")
    z, yh, k = s // 4, (s // 2) % 2, s % 2
    yl, x = c // 4, c % 4

    def seq_at(dz, dyh, dk):
        return ((z + dz + 4) % 4) * 4 + ((yh + dyh) % 2) * 2 + (k + dk) % 2

    def chan_at(dyl, dx):
        return ((yl + dyl) % 2) * 4 + (x + dx + 4) % 4

    def seq_dev(index):
        return {"seq": index, "chan": c}

    def chan_dev(index):
        return {"seq": s, "chan": index}

    z_up, z_down = seq_dev(seq_at(1, 0, 0)), seq_dev(seq_at(-1, 0, 0))
    y_far, mate = seq_dev(seq_at(0, 1, 0)), seq_dev(seq_at(0, 0, 1))
    x_up, x_down = chan_dev(chan_at(0, 1)), chan_dev(chan_at(0, -1))
    y_near = chan_dev(chan_at(1, 0))

    used = [6]

    def take():
        used[0] += 1
        return used[0] - 1

    def message(src, dst, device, kind, land=None):
        if kind in (SHARE, RESULT):
            land = kind
        return pltpu.make_async_remote_copy(
            src_ref=src, dst_ref=dst, send_sem=send_sem.at[kind],
            recv_sem=recv_sem.at[take() if land is None else land],
            device_id=device, device_id_type=MESH,
        )

    def send(src, dst, device, kind, land=None):
        copy = message(src, dst, device, kind, land)
        copy.start()
        return copy

    def drain(ref, sem):
        pltpu.make_async_copy(ref, ref, sem).wait()

    locals_started = []

    def fetch(src, dst):
        copy = pltpu.make_async_copy(src, dst, local_sem.at[len(locals_started)])
        copy.start()
        locals_started.append(copy)
        return copy

    barrier = pltpu.get_barrier_semaphore()
    sources = [chan_dev((c + i) % PEERS) for i in range(1, PEERS)]
    sources += [z_up, z_down, y_far, mate, seq_dev((s + GROUPS - 2) % GROUPS)]
    for device in sources:
        pl.semaphore_signal(barrier, inc=1, device_id=device, device_id_type=MESH)

    def cols(q):
        return pl.ds(q * PART, PART)

    def lag(n):
        return pl.ds((TAPS - n) * BLOCK, BLOCK)

    get_filters = fetch(filters, fbuf.at[pl.ds(BLOCK, TAPS * BLOCK)])
    get_forward = fetch(forward, tables)
    get_values = [fetch(values.at[:, cols(q)], xbuf.at[q, lag(0)]) for q in range(CHUNKS)]
    get_backward = fetch(backward, inverse)
    get_gates = fetch(gates, gbuf)

    def wcols(index):
        return pl.ds(pl.multiple_of(index * WIDTH, WIDTH), WIDTH)

    def rows_of(index):
        return pl.ds(pl.multiple_of(index * ROWS, ROWS), ROWS)

    get_weight = fetch(weight.at[:, wcols(c)], wbuf.at[s, rows_of(c)])

    edge = jnp.zeros((BLOCK, WIDTH), jnp.bfloat16)
    fbuf[:BLOCK, :] = edge
    fbuf[(TAPS + 1) * BLOCK :, :] = edge

    pl.semaphore_wait(barrier, len(sources))

    far, near, first, second = [], [], [], []
    straight = {}
    for q in DIRECT:
        straight[q] = message(values.at[:, cols(q)], xbuf.at[q, lag(2)], seq_dev((s + 2) % GROUPS), STRAIGHT)
        pl.when(s + 2 < GROUPS)(straight[q].start)
    for q in range(CHUNKS):
        copy = message(values.at[:, cols(q)], xbuf.at[q, lag(4)], z_up, FAR)
        pl.when(z < 3)(copy.start)
        far.append(copy)
        if q in DIRECT:
            copy = straight[q]
        else:
            src = pl.ds(pl.multiple_of((1 - yh) * TAPS * BLOCK, BLOCK), BLOCK)
            copy = message(xbuf.at[q, src], xbuf.at[q, lag(2)], y_far, NEAR)
        near.append(copy)
        src = pl.ds(pl.multiple_of((1 - k) * TAPS * BLOCK, BLOCK), BLOCK)
        dst = pl.ds(pl.multiple_of((3 - 2 * k) * BLOCK, BLOCK), BLOCK)
        first.append(message(xbuf.at[q, src], xbuf.at[q, dst], mate, FIRST))
        dst = pl.ds(pl.multiple_of((1 + 2 * k) * BLOCK, BLOCK), BLOCK)
        second.append(message(xbuf.at[q, lag(2)], xbuf.at[q, dst], mate, SECOND))
    others = [(1, 2), (1, 1), (1, -1), (0, 2), (1, 0), (0, 1), (0, -1)]
    for dyl, dx in others:
        peer = chan_at(dyl, dx)
        send(weight.at[:, wcols(peer)], wbuf.at[s, rows_of(c)], chan_dev(peer), SHARE)
    for q in range(CHUNKS):
        get_values[q].wait()
        if q not in DIRECT:
            pl.when(yh == 0)(near[q].start)
        pl.when(k == 0)(first[q].start)

    for n in range(1, TAPS + 1):

        @pl.when(s < n)
        def _():
            for q in range(CHUNKS):
                xbuf[q, lag(n), :] = jnp.zeros((BLOCK, PART), jnp.bfloat16)

    get_filters.wait()
    get_forward.wait()

    def spectrum(n, _):
        taps = fbuf[pl.ds(pl.multiple_of(n * BLOCK, BLOCK), 2 * BLOCK), :]
        kern[n] = dot(tables[...], taps)
        return 0

    lax.fori_loop(0, TAPS + 1, spectrum, 0)
    for q in range(CHUNKS):
        zbuf[0, :, cols(q)] = dot(tables[:, :BLOCK], xbuf[q, lag(0), :])

    def begin(i, _):
        re = pl.ds(pl.multiple_of(i * STRIP, STRIP), STRIP)
        im = pl.ds(pl.multiple_of(i * STRIP + BLOCK, STRIP), STRIP)
        kr, ki = kern[0, re, :], kern[0, im, :]
        wr, wi = zbuf[0, re, :], zbuf[0, im, :]
        total[re, :] = kr * wr - ki * wi
        total[im, :] = kr * wi + ki * wr
        return 0

    lax.fori_loop(0, BLOCK // STRIP, begin, 0)
    get_backward.wait()
    get_gates.wait()

    def wpiece(dz, dyh):
        return wbuf.at[seq_at(dz, dyh, 0)]

    def whalf(dz, dyh, lower):
        return wbuf.at[seq_at(dz, dyh, 0), pl.ds(HALF * lower, HALF)]


    def to_mate(dz, dyh):
        send(wpiece(dz, dyh), wpiece(dz, dyh), mate, WEIGHT, MATES + dyh)

    def forward_far(q):
        pl.when(z > 0)(far[q].wait_recv)
        if q not in DIRECT:
            pl.when((yh == 1) & (z > 0))(near[q].start)
        pl.when((k == 1) & (z > 0))(first[q].start)

    def mates(q):
        @pl.when(s >= 2)
        def _():
            near[q].wait_recv()
            second[q].start()

    def convolve(q):
        pl.when((k == 1) | (z > 0))(first[q].wait_recv)
        pl.when(s >= 2)(second[q].wait_recv)
        for n in range(1, TAPS + 1):
            zbuf[n, :, cols(q)] = dot(tables[:, :BLOCK], xbuf[q, lag(n), :])

        def combine(i, _):
            re = pl.ds(pl.multiple_of(i * STRIP, STRIP), STRIP)
            im = pl.ds(pl.multiple_of(i * STRIP + BLOCK, STRIP), STRIP)
            real, imag = total[re, cols(q)], total[im, cols(q)]
            for n in range(1, TAPS + 1):
                kr, ki = kern[n, re, cols(q)], kern[n, im, cols(q)]
                wr, wi = zbuf[n, re, cols(q)], zbuf[n, im, cols(q)]
                real = real + kr * wr - ki * wi
                imag = imag + kr * wi + ki * wr
            ybuf[re, :] = real.astype(jnp.bfloat16)
            ybuf[im, :] = imag.astype(jnp.bfloat16)
            return 0

        lax.fori_loop(0, BLOCK // STRIP, combine, 0)
        now = xbuf[q, lag(0), :].astype(jnp.float32)
        filtered = dot(inverse[...], ybuf[...]) + skip[:, cols(q)] * now
        abuf[c, :, cols(q)] = (gbuf[:, cols(q)].astype(jnp.float32) * filtered).astype(jnp.bfloat16)

    def apiece(q, dyl, dx):
        return abuf.at[chan_at(dyl, dx), :, cols(q)]

    def ahalf(q, dyl, dx, lower):
        return abuf.at[chan_at(dyl, dx), pl.ds(HALF * lower, HALF), cols(q)]

    def same(ref, device, kind=WEIGHT):
        return send(ref, ref, device, kind)

    def gate(ref, device, land=None):
        return send(ref, ref, device, GATED, land)

    a_up, a_down, a_near = [], [], []

    def spread(q):
        a_up.append(gate(apiece(q, 0, 0), x_up))
        a_down.append(gate(apiece(q, 0, 0), x_down))
        a_near.append(gate(apiece(q, 0, 0), y_near))

    a_up2, a_down2 = [], []

    def relay(q):
        a_up[q].wait_recv()
        a_up2.append(gate(ahalf(q, 0, -1, 0), x_up))
        a_down[q].wait_recv()
        a_down2.append(gate(ahalf(q, 0, 1, 1), x_down))
        a_near[q].wait_recv()
        gate(apiece(q, 1, 0), x_up, RELAYED)
        gate(apiece(q, 1, 0), x_down, RELAYED)

    def relay_far(q):
        a_up2[q].wait_recv()
        a_down2[q].wait_recv()
        gate(apiece(q, 0, 2), y_near, ACROSS)

    w = {}

    def both(dz, dyh, device, order):
        return [same(whalf(dz, dyh, lower), device) for lower in order]

    def ready(name):
        for copy in w[name]:
            copy.wait_recv()

    def w_own():
        get_weight.wait()
        drain(wbuf.at[0, pl.ds(0, BLOCK - ROWS)], recv_sem.at[SHARE])
        w["up"] = both(0, 0, z_up, (0, 1))
        w["down"] = both(0, 0, z_down, (1, 0))
        to_mate(0, 0)

    def wquarter(i):
        return wbuf.at[seq_at(0, 0, 0), pl.ds(i * QUARTER, QUARTER)]

    def wother(i):
        return wbuf.at[seq_at(0, 1, 0), pl.ds(i * QUARTER, QUARTER)]

    w["far"], w["fup"], w["fdown"] = [], [], []

    def w_cross(i):
        w["far"].append(same(wquarter(i), y_far))

    def w_relay():
        w["down"].pop(0).wait_recv()
        w["down2"] = same(whalf(1, 0, 1), z_down)
        w["up"].pop(0).wait_recv()
        w["up2"] = same(whalf(-1, 0, 0), z_up)

    def w_mates():
        ready("down")
        to_mate(1, 0)
        ready("up")
        to_mate(-1, 0)

    def w_other(i):
        w["far"][i].wait_recv()
        w["fup"].append(same(wother(i), z_up))
        w["fdown"].append(same(wother(i), z_down))
        if i == 3:
            to_mate(0, 1)

    def w_two():
        w["down2"].wait_recv()
        w["up2"].wait_recv()
        to_mate(2, 0)

    def wnext(dz, i):
        return wbuf.at[seq_at(dz, 1, 0), pl.ds(i * QUARTER, QUARTER)]

    w["fup2"], w["fdown2"] = [], []

    def w_relay_up(i):
        w["fup"][i].wait_recv()
        w["fup2"].append(same(wnext(-1, i), z_up))

    def w_relay_down(i):
        w["fdown"][i].wait_recv()
        w["fdown2"].append(same(wnext(1, i), z_down))

    def w_mates_other():
        for copy in w["fdown"][:2]:
            copy.wait_recv()
        to_mate(1, 1)
        for copy in w["fup"][2:]:
            copy.wait_recv()
        to_mate(-1, 1)

    def w_last():
        for copy in w["fup2"]:
            copy.wait_recv()
        last = [same(whalf(2, 1, 0), mate)]
        for copy in w["fdown2"]:
            copy.wait_recv()
        last.append(same(whalf(2, 1, 1), mate))
        return last

    for step in SCHEDULE:
        name, *rest = step
        {
            "f": forward_far, "n": mates, "c": convolve, "s": spread, "r": relay, "R": relay_far,
            "own": w_own, "x": w_cross, "wr": w_relay, "o": w_other, "w2": w_two,
            "u": w_relay_up, "d": w_relay_down, "wm": w_mates, "wmo": w_mates_other,
        }[name](*rest)
    def project(origin):
        acc[...] += dot(abuf[origin], wbuf[pl.ds(2 * origin, 2)].reshape(WIDTH, WIDTH))

    assert used[0] + 2 == ARRIVALS, used
    acc[...] = jnp.zeros_like(acc)
    last_a = chan_at(1, 2)
    last_w = seq_at(2, 1, 0) // 2

    def group(first):
        for step in (0, 2):
            origin = first + step
            pl.when((origin != last_a) & (origin != last_w))(functools.partial(project, origin))

    def wait_all(copies):
        for copy in copies:
            copy.wait_recv()

    drain(wbuf.at[pl.ds(0, 4)], recv_sem.at[MATES])
    group(4 * yl + yh)
    final = w_last()
    drain(wbuf.at[pl.ds(0, 3)], recv_sem.at[MATES + 1])
    group(4 * yl + 1 - yh)
    drain(wbuf.at[pl.ds(0, 2)], recv_sem.at[RELAYED])
    group(4 * (1 - yl) + yh)
    group(4 * (1 - yl) + 1 - yh)
    drain(wbuf.at[0], recv_sem.at[ACROSS])
    pl.when(last_a != last_w)(functools.partial(project, last_a))
    wait_all(final)
    project(last_w)
    obuf[...] = acc[...].astype(jnp.bfloat16)
    mine = pltpu.make_async_copy(
        obuf.at[rows_of(c)], out.at[:, wcols(c)], local_sem.at[len(locals_started)]
    )
    mine.start()
    for dyl, dx in others:
        peer = chan_at(dyl, dx)
        send(obuf.at[rows_of(peer)], out.at[:, wcols(c)], chan_dev(peer), RESULT)
    def settle(condition, kind, rows):
        pl.when(condition)(lambda: drain(wbuf.at[0, pl.ds(0, rows)], send_sem.at[kind]))

    per = BLOCK // CHUNKS
    settle(z < 3, FAR, BLOCK)
    settle((k == 0) | (z > 0), FIRST, BLOCK)
    settle(s >= 2, SECOND, BLOCK)
    settle((yh == 0) | (z > 0), NEAR, BLOCK - per * len(DIRECT))
    settle(s + 2 < GROUPS, STRAIGHT, per * len(DIRECT))
    part = wbuf.at[0, pl.ds(0, BLOCK - ROWS)]
    drain(part, send_sem.at[SHARE])
    drain(wbuf.at[pl.ds(0, 15)], send_sem.at[WEIGHT])
    drain(wbuf.at[pl.ds(0, 7)], send_sem.at[GATED])
    drain(part, send_sem.at[RESULT])
    mine.wait()
    drain(part, recv_sem.at[RESULT])


SENDS = 9
ARRIVALS = 6 + 4 * CHUNKS + 24 + 5 * CHUNKS


def body(values, gates, filters, skip, out_weight):
    forward, backward = dft_tables(BLOCK)
    forward = jnp.asarray(forward, jnp.bfloat16)
    backward = jnp.asarray(backward, jnp.bfloat16)
    anywhere = pl.BlockSpec(memory_space=pl.ANY)
    local = pl.BlockSpec(memory_space=pltpu.VMEM)
    bf16, f32 = jnp.bfloat16, jnp.float32
    return pl.pallas_call(
        kernel,
        out_shape=jax.ShapeDtypeStruct((ROWS, PEERS * WIDTH), bf16),
        in_specs=[anywhere, anywhere, anywhere, local, anywhere, anywhere, anywhere],
        out_specs=anywhere,
        scratch_shapes=[
            pltpu.VMEM((CHUNKS, (TAPS + 1) * BLOCK, PART), bf16),
            pltpu.VMEM((BLOCK, WIDTH), bf16),
            pltpu.VMEM(((TAPS + 2) * BLOCK, WIDTH), bf16),
            pltpu.VMEM((2 * BLOCK, 2 * BLOCK), bf16),
            pltpu.VMEM((BLOCK, 2 * BLOCK), bf16),
            pltpu.VMEM((TAPS + 1, 2 * BLOCK, WIDTH), f32),
            pltpu.VMEM((TAPS + 1, 2 * BLOCK, WIDTH), f32),
            pltpu.VMEM((2 * BLOCK, WIDTH), f32),
            pltpu.VMEM((2 * BLOCK, PART), bf16),
            pltpu.VMEM((PEERS, BLOCK, WIDTH), bf16),
            pltpu.VMEM((GROUPS, BLOCK, WIDTH), bf16),
            pltpu.VMEM((BLOCK, WIDTH), f32),
            pltpu.VMEM((BLOCK, WIDTH), bf16),
            pltpu.SemaphoreType.DMA((SENDS,)),
            pltpu.SemaphoreType.DMA((ARRIVALS,)),
            pltpu.SemaphoreType.DMA((10,)),
        ],
        compiler_params=pltpu.CompilerParams(
            collective_id=0, has_side_effects=True, vmem_limit_bytes=60 * 1024 * 1024
        ),
    )(values, gates, filters, skip.reshape(1, -1), out_weight, forward, backward)


def solution(mesh):
    in_specs = (
        P("seq", "chan"),
        P("seq", "chan"),
        P(None, "chan"),
        P("chan"),
        P(("seq", "chan"), None),
    )
    out_specs = P(("seq", "chan"), None)
    return jax.shard_map(body, mesh=mesh, in_specs=in_specs, out_specs=out_specs, check_vma=False)
```

```python
import functools

import numpy as np

import jax
import jax.numpy as jnp
from jax import lax
from jax.experimental import pallas as pl
from jax.experimental.pallas import tpu as pltpu
from jax.sharding import PartitionSpec as P

MESH = pl.DeviceIdType.MESH
CHUNKS = 4
BLOCK = 256
WIDTH = 512
PART = WIDTH // CHUNKS
TAPS = 4
PEERS = 8
GROUPS = 16
ROWS = 32
HALF = BLOCK // 2
QUARTER = BLOCK // 4
STRIP = 32
SHARE, RESULT, WEIGHT, GATED, FAR, FIRST, SECOND, NEAR, STRAIGHT = range(9)
RELAYED, ACROSS, MATES = 2, 3, 4
DIRECT = (0,)
SCHEDULE = (
    ("f", 0), ("f", 1), ("n", 0), ("own",), ("x", 0), ("f", 2),
    ("c", 0), ("s", 0), ("x", 1), ("f", 3), ("n", 1), ("x", 2),
    ("c", 1), ("s", 1), ("x", 3), ("n", 2), ("r", 0), ("wr",),
    ("o", 0), ("c", 2), ("s", 2), ("n", 3), ("o", 1), ("c", 3),
    ("s", 3), ("r", 1), ("wm",), ("o", 2), ("r", 2), ("o", 3),
    ("u", 0), ("R", 0), ("u", 1), ("w2",), ("d", 2), ("r", 3),
    ("R", 1), ("R", 2), ("d", 3), ("R", 3), ("wmo",),
)


def dft_tables(block):
    size = 2 * block
    freq = (np.arange(block) + 0.5)[:, None]
    angle = 2.0 * np.pi * freq * np.arange(size)[None, :] / size
    forward = np.concatenate([np.cos(angle), -np.sin(angle)], axis=0)
    late = angle[:, block:]
    backward = np.concatenate([np.cos(late), -np.sin(late)], axis=0).T / block
    return forward, backward


def dot(a, b):
    return jnp.dot(a, b, preferred_element_type=jnp.float32)


def kernel(
    values, gates, filters, skip, weight, forward, backward, out,
    xbuf, gbuf, fbuf, tables, inverse, kern, zbuf, total, ybuf, abuf, wbuf, acc, obuf,
    send_sem, recv_sem, local_sem,
):
    s = lax.axis_index("seq")
    c = lax.axis_index("chan")
    z, yh, k = s // 4, (s // 2) % 2, s % 2
    yl, x = c // 4, c % 4

    def seq_at(dz, dyh, dk):
        return ((z + dz + 4) % 4) * 4 + ((yh + dyh) % 2) * 2 + (k + dk) % 2

    def chan_at(dyl, dx):
        return ((yl + dyl) % 2) * 4 + (x + dx + 4) % 4

    def seq_dev(index):
        return {"seq": index, "chan": c}

    def chan_dev(index):
        return {"seq": s, "chan": index}

    z_up, z_down = seq_dev(seq_at(1, 0, 0)), seq_dev(seq_at(-1, 0, 0))
    y_far, mate = seq_dev(seq_at(0, 1, 0)), seq_dev(seq_at(0, 0, 1))
    x_up, x_down = chan_dev(chan_at(0, 1)), chan_dev(chan_at(0, -1))
    y_near = chan_dev(chan_at(1, 0))

    used = [6]

    def take():
        used[0] += 1
        return used[0] - 1

    def message(src, dst, device, kind, land=None):
        if kind in (SHARE, RESULT):
            land = kind
        return pltpu.make_async_remote_copy(
            src_ref=src, dst_ref=dst, send_sem=send_sem.at[kind],
            recv_sem=recv_sem.at[take() if land is None else land],
            device_id=device, device_id_type=MESH,
        )

    def send(src, dst, device, kind, land=None):
        copy = message(src, dst, device, kind, land)
        copy.start()
        return copy

    def drain(ref, sem):
        pltpu.make_async_copy(ref, ref, sem).wait()

    locals_started = []

    def fetch(src, dst):
        copy = pltpu.make_async_copy(src, dst, local_sem.at[len(locals_started)])
        copy.start()
        locals_started.append(copy)
        return copy

    barrier = pltpu.get_barrier_semaphore()
    sources = [chan_dev((c + i) % PEERS) for i in range(1, PEERS)]
    sources += [z_up, z_down, y_far, mate, seq_dev((s + GROUPS - 2) % GROUPS)]
    for device in sources:
        pl.semaphore_signal(barrier, inc=1, device_id=device, device_id_type=MESH)

    def cols(q):
        return pl.ds(q * PART, PART)

    def lag(n):
        return pl.ds((TAPS - n) * BLOCK, BLOCK)

    get_filters = fetch(filters, fbuf.at[pl.ds(BLOCK, TAPS * BLOCK)])
    get_forward = fetch(forward, tables)
    get_values = [fetch(values.at[:, cols(q)], xbuf.at[q, lag(0)]) for q in range(CHUNKS)]
    get_backward = fetch(backward, inverse)
    get_gates = fetch(gates, gbuf)

    def wcols(index):
        return pl.ds(pl.multiple_of(index * WIDTH, WIDTH), WIDTH)

    def rows_of(index):
        return pl.ds(pl.multiple_of(index * ROWS, ROWS), ROWS)

    get_weight = fetch(weight.at[:, wcols(c)], wbuf.at[s, rows_of(c)])

    edge = jnp.zeros((BLOCK, WIDTH), jnp.bfloat16)
    fbuf[:BLOCK, :] = edge
    fbuf[(TAPS + 1) * BLOCK :, :] = edge

    pl.semaphore_wait(barrier, len(sources))

    far, near, first, second = [], [], [], []
    straight = {}
    for q in DIRECT:
        straight[q] = message(values.at[:, cols(q)], xbuf.at[q, lag(2)], seq_dev((s + 2) % GROUPS), STRAIGHT)
        pl.when(s + 2 < GROUPS)(straight[q].start)
    for q in range(CHUNKS):
        copy = message(values.at[:, cols(q)], xbuf.at[q, lag(4)], z_up, FAR)
        pl.when(z < 3)(copy.start)
        far.append(copy)
        if q in DIRECT:
            copy = straight[q]
        else:
            src = pl.ds(pl.multiple_of((1 - yh) * TAPS * BLOCK, BLOCK), BLOCK)
            copy = message(xbuf.at[q, src], xbuf.at[q, lag(2)], y_far, NEAR)
        near.append(copy)
        src = pl.ds(pl.multiple_of((1 - k) * TAPS * BLOCK, BLOCK), BLOCK)
        dst = pl.ds(pl.multiple_of((3 - 2 * k) * BLOCK, BLOCK), BLOCK)
        first.append(message(xbuf.at[q, src], xbuf.at[q, dst], mate, FIRST))
        dst = pl.ds(pl.multiple_of((1 + 2 * k) * BLOCK, BLOCK), BLOCK)
        second.append(message(xbuf.at[q, lag(2)], xbuf.at[q, dst], mate, SECOND))
    others = [(1, 2), (1, 1), (1, -1), (0, 2), (1, 0), (0, 1), (0, -1)]
    for dyl, dx in others:
        peer = chan_at(dyl, dx)
        send(weight.at[:, wcols(peer)], wbuf.at[s, rows_of(c)], chan_dev(peer), SHARE)
    for q in range(CHUNKS):
        get_values[q].wait()
        if q not in DIRECT:
            pl.when(yh == 0)(near[q].start)
        pl.when(k == 0)(first[q].start)

    for n in range(1, TAPS + 1):

        @pl.when(s < n)
        def _():
            for q in range(CHUNKS):
                xbuf[q, lag(n), :] = jnp.zeros((BLOCK, PART), jnp.bfloat16)

    get_filters.wait()
    get_forward.wait()

    def spectrum(n, _):
        taps = fbuf[pl.ds(pl.multiple_of(n * BLOCK, BLOCK), 2 * BLOCK), :]
        kern[n] = dot(tables[...], taps)
        return 0

    lax.fori_loop(0, TAPS + 1, spectrum, 0)
    for q in range(CHUNKS):
        zbuf[0, :, cols(q)] = dot(tables[:, :BLOCK], xbuf[q, lag(0), :])

    def begin(i, _):
        re = pl.ds(pl.multiple_of(i * STRIP, STRIP), STRIP)
        im = pl.ds(pl.multiple_of(i * STRIP + BLOCK, STRIP), STRIP)
        kr, ki = kern[0, re, :], kern[0, im, :]
        wr, wi = zbuf[0, re, :], zbuf[0, im, :]
        total[re, :] = kr * wr - ki * wi
        total[im, :] = kr * wi + ki * wr
        return 0

    lax.fori_loop(0, BLOCK // STRIP, begin, 0)
    get_backward.wait()
    get_gates.wait()

    def wpiece(dz, dyh):
        return wbuf.at[seq_at(dz, dyh, 0)]

    def whalf(dz, dyh, lower):
        return wbuf.at[seq_at(dz, dyh, 0), pl.ds(HALF * lower, HALF)]


    def to_mate(dz, dyh):
        send(wpiece(dz, dyh), wpiece(dz, dyh), mate, WEIGHT, MATES + dyh)

    def forward_far(q):
        pl.when(z > 0)(far[q].wait_recv)
        if q not in DIRECT:
            pl.when((yh == 1) & (z > 0))(near[q].start)
        pl.when((k == 1) & (z > 0))(first[q].start)

    def mates(q):
        @pl.when(s >= 2)
        def _():
            near[q].wait_recv()
            second[q].start()

    def convolve(q):
        pl.when((k == 1) | (z > 0))(first[q].wait_recv)
        pl.when(s >= 2)(second[q].wait_recv)
        for n in range(1, TAPS + 1):
            zbuf[n, :, cols(q)] = dot(tables[:, :BLOCK], xbuf[q, lag(n), :])

        def combine(i, _):
            re = pl.ds(pl.multiple_of(i * STRIP, STRIP), STRIP)
            im = pl.ds(pl.multiple_of(i * STRIP + BLOCK, STRIP), STRIP)
            real, imag = total[re, cols(q)], total[im, cols(q)]
            for n in range(1, TAPS + 1):
                kr, ki = kern[n, re, cols(q)], kern[n, im, cols(q)]
                wr, wi = zbuf[n, re, cols(q)], zbuf[n, im, cols(q)]
                real = real + kr * wr - ki * wi
                imag = imag + kr * wi + ki * wr
            ybuf[re, :] = real.astype(jnp.bfloat16)
            ybuf[im, :] = imag.astype(jnp.bfloat16)
            return 0

        lax.fori_loop(0, BLOCK // STRIP, combine, 0)
        now = xbuf[q, lag(0), :].astype(jnp.float32)
        filtered = dot(inverse[...], ybuf[...]) + skip[:, cols(q)] * now
        abuf[c, :, cols(q)] = (gbuf[:, cols(q)].astype(jnp.float32) * filtered).astype(jnp.bfloat16)

    def apiece(q, dyl, dx):
        return abuf.at[chan_at(dyl, dx), :, cols(q)]

    def ahalf(q, dyl, dx, lower):
        return abuf.at[chan_at(dyl, dx), pl.ds(HALF * lower, HALF), cols(q)]

    def same(ref, device, kind=WEIGHT):
        return send(ref, ref, device, kind)

    def gate(ref, device, land=None):
        return send(ref, ref, device, GATED, land)

    a_up, a_down, a_near = [], [], []

    def spread(q):
        a_up.append(gate(apiece(q, 0, 0), x_up))
        a_down.append(gate(apiece(q, 0, 0), x_down))
        a_near.append(gate(apiece(q, 0, 0), y_near))

    a_up2, a_down2 = [], []

    def relay(q):
        a_up[q].wait_recv()
        a_up2.append(gate(ahalf(q, 0, -1, 0), x_up))
        a_down[q].wait_recv()
        a_down2.append(gate(ahalf(q, 0, 1, 1), x_down))
        a_near[q].wait_recv()
        gate(apiece(q, 1, 0), x_up, RELAYED)
        gate(apiece(q, 1, 0), x_down, RELAYED)

    def relay_far(q):
        a_up2[q].wait_recv()
        a_down2[q].wait_recv()
        gate(apiece(q, 0, 2), y_near, ACROSS)

    w = {}

    def both(dz, dyh, device, order):
        return [same(whalf(dz, dyh, lower), device) for lower in order]

    def ready(name):
        for copy in w[name]:
            copy.wait_recv()

    def w_own():
        get_weight.wait()
        drain(wbuf.at[0, pl.ds(0, BLOCK - ROWS)], recv_sem.at[SHARE])
        w["up"] = both(0, 0, z_up, (0, 1))
        w["down"] = both(0, 0, z_down, (1, 0))
        to_mate(0, 0)

    def wquarter(i):
        return wbuf.at[seq_at(0, 0, 0), pl.ds(i * QUARTER, QUARTER)]

    def wother(i):
        return wbuf.at[seq_at(0, 1, 0), pl.ds(i * QUARTER, QUARTER)]

    w["far"], w["fup"], w["fdown"] = [], [], []

    def w_cross(i):
        w["far"].append(same(wquarter(i), y_far))

    def w_relay():
        w["down"].pop(0).wait_recv()
        w["down2"] = same(whalf(1, 0, 1), z_down)
        w["up"].pop(0).wait_recv()
        w["up2"] = same(whalf(-1, 0, 0), z_up)

    def w_mates():
        ready("down")
        to_mate(1, 0)
        ready("up")
        to_mate(-1, 0)

    def w_other(i):
        w["far"][i].wait_recv()
        w["fup"].append(same(wother(i), z_up))
        w["fdown"].append(same(wother(i), z_down))
        if i == 3:
            to_mate(0, 1)

    def w_two():
        w["down2"].wait_recv()
        w["up2"].wait_recv()
        to_mate(2, 0)

    def wnext(dz, i):
        return wbuf.at[seq_at(dz, 1, 0), pl.ds(i * QUARTER, QUARTER)]

    w["fup2"], w["fdown2"] = [], []

    def w_relay_up(i):
        w["fup"][i].wait_recv()
        w["fup2"].append(same(wnext(-1, i), z_up))

    def w_relay_down(i):
        w["fdown"][i].wait_recv()
        w["fdown2"].append(same(wnext(1, i), z_down))

    def w_mates_other():
        for copy in w["fdown"][:2]:
            copy.wait_recv()
        to_mate(1, 1)
        for copy in w["fup"][2:]:
            copy.wait_recv()
        to_mate(-1, 1)

    def w_last():
        for copy in w["fup2"]:
            copy.wait_recv()
        last = [same(whalf(2, 1, 0), mate)]
        for copy in w["fdown2"]:
            copy.wait_recv()
        last.append(same(whalf(2, 1, 1), mate))
        return last

    for step in SCHEDULE:
        name, *rest = step
        {
            "f": forward_far, "n": mates, "c": convolve, "s": spread, "r": relay, "R": relay_far,
            "own": w_own, "x": w_cross, "wr": w_relay, "o": w_other, "w2": w_two,
            "u": w_relay_up, "d": w_relay_down, "wm": w_mates, "wmo": w_mates_other,
        }[name](*rest)
    def project(origin):
        acc[...] += dot(abuf[origin], wbuf[pl.ds(2 * origin, 2)].reshape(WIDTH, WIDTH))

    assert used[0] + 2 == ARRIVALS, used
    acc[...] = jnp.zeros_like(acc)
    last_a = chan_at(1, 2)
    last_w = seq_at(2, 1, 0) // 2

    def group(first):
        for step in (0, 2):
            origin = first + step
            pl.when((origin != last_a) & (origin != last_w))(functools.partial(project, origin))

    def wait_all(copies):
        for copy in copies:
            copy.wait_recv()

    drain(wbuf.at[pl.ds(0, 4)], recv_sem.at[MATES])
    group(4 * yl + yh)
    final = w_last()
    drain(wbuf.at[pl.ds(0, 3)], recv_sem.at[MATES + 1])
    group(4 * yl + 1 - yh)
    drain(wbuf.at[pl.ds(0, 2)], recv_sem.at[RELAYED])
    group(4 * (1 - yl) + yh)
    group(4 * (1 - yl) + 1 - yh)
    drain(wbuf.at[0], recv_sem.at[ACROSS])
    pl.when(last_a != last_w)(functools.partial(project, last_a))
    wait_all(final)
    term = dot(abuf[last_w], wbuf[pl.ds(2 * last_w, 2)].reshape(WIDTH, WIDTH))
    obuf[...] = (acc[...] + term).astype(jnp.bfloat16)
    mine = pltpu.make_async_copy(
        obuf.at[rows_of(c)], out.at[:, wcols(c)], local_sem.at[len(locals_started)]
    )
    mine.start()
    for dyl, dx in others:
        peer = chan_at(dyl, dx)
        send(obuf.at[rows_of(peer)], out.at[:, wcols(c)], chan_dev(peer), RESULT)
    def settle(condition, kind, rows):
        pl.when(condition)(lambda: drain(wbuf.at[0, pl.ds(0, rows)], send_sem.at[kind]))

    per = BLOCK // CHUNKS
    settle(z < 3, FAR, BLOCK)
    settle((k == 0) | (z > 0), FIRST, BLOCK)
    settle(s >= 2, SECOND, BLOCK)
    settle((yh == 0) | (z > 0), NEAR, BLOCK - per * len(DIRECT))
    settle(s + 2 < GROUPS, STRAIGHT, per * len(DIRECT))
    part = wbuf.at[0, pl.ds(0, BLOCK - ROWS)]
    drain(part, send_sem.at[SHARE])
    drain(wbuf.at[pl.ds(0, 15)], send_sem.at[WEIGHT])
    drain(wbuf.at[pl.ds(0, 7)], send_sem.at[GATED])
    drain(part, send_sem.at[RESULT])
    mine.wait()
    drain(part, recv_sem.at[RESULT])


SENDS = 9
ARRIVALS = 6 + 4 * CHUNKS + 24 + 5 * CHUNKS


def body(values, gates, filters, skip, out_weight):
    forward, backward = dft_tables(BLOCK)
    forward = jnp.asarray(forward, jnp.bfloat16)
    backward = jnp.asarray(backward, jnp.bfloat16)
    anywhere = pl.BlockSpec(memory_space=pl.ANY)
    local = pl.BlockSpec(memory_space=pltpu.VMEM)
    bf16, f32 = jnp.bfloat16, jnp.float32
    return pl.pallas_call(
        kernel,
        out_shape=jax.ShapeDtypeStruct((ROWS, PEERS * WIDTH), bf16),
        in_specs=[anywhere, anywhere, anywhere, local, anywhere, anywhere, anywhere],
        out_specs=anywhere,
        scratch_shapes=[
            pltpu.VMEM((CHUNKS, (TAPS + 1) * BLOCK, PART), bf16),
            pltpu.VMEM((BLOCK, WIDTH), bf16),
            pltpu.VMEM(((TAPS + 2) * BLOCK, WIDTH), bf16),
            pltpu.VMEM((2 * BLOCK, 2 * BLOCK), bf16),
            pltpu.VMEM((BLOCK, 2 * BLOCK), bf16),
            pltpu.VMEM((TAPS + 1, 2 * BLOCK, WIDTH), f32),
            pltpu.VMEM((TAPS + 1, 2 * BLOCK, WIDTH), f32),
            pltpu.VMEM((2 * BLOCK, WIDTH), f32),
            pltpu.VMEM((2 * BLOCK, PART), bf16),
            pltpu.VMEM((PEERS, BLOCK, WIDTH), bf16),
            pltpu.VMEM((GROUPS, BLOCK, WIDTH), bf16),
            pltpu.VMEM((BLOCK, WIDTH), f32),
            pltpu.VMEM((BLOCK, WIDTH), bf16),
            pltpu.SemaphoreType.DMA((SENDS,)),
            pltpu.SemaphoreType.DMA((ARRIVALS,)),
            pltpu.SemaphoreType.DMA((10,)),
        ],
        compiler_params=pltpu.CompilerParams(
            collective_id=0, has_side_effects=True, vmem_limit_bytes=60 * 1024 * 1024
        ),
    )(values, gates, filters, skip.reshape(1, -1), out_weight, forward, backward)


def solution(mesh):
    in_specs = (
        P("seq", "chan"),
        P("seq", "chan"),
        P(None, "chan"),
        P("chan"),
        P(("seq", "chan"), None),
    )
    out_specs = P(("seq", "chan"), None)
    return jax.shard_map(body, mesh=mesh, in_specs=in_specs, out_specs=out_specs, check_vma=False)
```
